32 devices in a mesh: context: 4 (over z), tensor: 2 (over core), dp: 4 (over y, x).
Axes of the slice: x: 2, y: 2, z: 4, core: 2. Of those that a mesh axis runs over, the one named last changes fastest.
Arguments:
- queries: bfloat16 [4, 3072, 2048], P('dp', 'context', 'tensor'), may hold values from -1.75 to 1.75
- keys_in: bfloat16 [4, 3072, 2048], P('dp', 'context', 'tensor'), may hold values from -1.75 to 1.75
- values: bfloat16 [4, 3072, 2048], P('dp', 'context', 'tensor'), may hold values from -48 to 48
- norm_gain: float32 [2048], P('tensor'), may hold values from 0.25 to 1.75
- segment_ids: int32 [4, 48], P('dp', 'context'), may hold values from 0 to 5, never falling along the last dimension, each value on 1 to 24 neighbouring positions
- grad_out: bfloat16 [4, 3072, 2048], P('dp', 'context', 'tensor'), may hold values from -8 to 8
Outputs:
- normed_out: bfloat16 [4, 3072, 2048], P('dp', 'context', 'tensor')
- grad_queries: bfloat16 [4, 3072, 2048], P('dp', 'context', 'tensor')
- grad_keys: bfloat16 [4, 3072, 2048], P('dp', 'context', 'tensor')
- grad_values: bfloat16 [4, 3072, 2048], P('dp', 'context', 'tensor')
- grad_gain: float32 [2048], P('tensor')
The draws below stay inside these ranges and needn't reach their ends.
Inputs may be any that keep to these rules, and one draw needn't show every extreme that they name: `segment_ids`: along each sequence the ids never fall; each id is one document.
All inputs are finite; a program needn't handle non-finite values.
Results may differ from the reference program's by a relative error of at most 0.0057.
Values sent between devices are 32-bit elements; how exact they have to be, the bound alone decides.
A program may use at most 128 MiB of HBM per device.

```python
import math
import jax
import jax.numpy as jnp
import numpy as np
from jax import lax

HEADS = 16
HD = 128
BLK = 256
SEGB = 64
WIDTH = 2048
SEQ = 3072
NBLK = 48
BATCH = 4


def draw_values(key, part):
    key_base, key_cols, key_rows = jax.random.split(key, 3)
    col_scale = jnp.exp(jax.random.uniform(key_cols, (WIDTH,), jnp.float32, math.log(0.3), math.log(3.0)))
    row_scale = jnp.exp(jax.random.uniform(key_rows, (BATCH, SEQ, 1), jnp.float32, math.log(0.4), math.log(4.0)))
    base = jnp.clip(jax.random.normal(key_base, (BATCH, SEQ, WIDTH), jnp.float32), -4.0, 4.0)
    return (base * col_scale * row_scale).astype(jnp.bfloat16)


def draw_grad_out(key, part):
    key_base = jax.random.fold_in(key, 0)
    position = (jnp.arange(SEQ, dtype=jnp.float32) + 0.5) / SEQ
    base = jnp.clip(jax.random.normal(key_base, (BATCH, SEQ, WIDTH), jnp.float32), -4.0, 4.0)
    scale = 0.5 + 1.5 * position
    result = base * scale[None, :, None]
    return result.astype(jnp.bfloat16)


def levels(stream_key, extent, cuts, least, high):
    gain = 1.0
    for dim, shards_of in cuts:
        heights = jax.random.uniform(jax.random.fold_in(jax.random.fold_in(stream_key, 6), dim), (shards_of,), jnp.float32, least / len(cuts), high / len(cuts))
        gain = gain * jnp.repeat(jnp.exp(heights), extent[dim] // shards_of).reshape((-1,) + (1,) * (len(extent) - 1 - dim))
    return gain


def split_up(amount, total, limit, lean):
    loads = [(1 << 20) // math.isqrt(rank ** lean) + 1 for rank in range(2, amount + 1)]
    spare, given = total - limit - (amount - 1), [1] * (amount - 1)
    while spare > 0:
        movable = [i for i in range(amount - 1) if given[i] < limit]
        mass, budget = sum([loads[i] for i in movable]), spare
        for i in movable:
            more = min(limit - given[i], max(1, budget * loads[i] // mass), spare)
            given[i] = given[i] + more
            spare = spare - more
    return np.array([limit] + given)


def uneven(own_key, number_of, total, bound, skew):
    if number_of == 2:
        one = jax.random.randint(own_key, (), max(1, total - bound), min(bound, total - 1) + 1)
        return jnp.stack([one, total - one])
    sizes = jnp.asarray(split_up(number_of, total, bound, skew), jnp.int32)
    pairs = (number_of - 1) // 2
    source_of, taker = sizes[1:1 + 2 * pairs:2], sizes[2:2 + 2 * pairs:2]
    slack = jnp.minimum(source_of - 1, bound - taker)
    shifted = jax.random.randint(jax.random.fold_in(own_key, 1), (pairs,), 0, 1 << 20) % (slack + 1)
    sizes = sizes.at[1:1 + 2 * pairs:2].set(source_of - shifted).at[2:2 + 2 * pairs:2].set(taker + shifted)
    return sizes[jax.random.permutation(jax.random.fold_in(own_key, 2), number_of)]


def bell_draw(key, shape, spread, reach, cuts=(), kind=jnp.bfloat16):
    factor_of = levels(key, shape, cuts, -0.22, 0.18) if cuts else 1.0
    entries = jax.random.normal(key, shape, jnp.float32) * spread * factor_of
    return jnp.minimum(jnp.maximum(entries, -reach), reach).astype(kind)


def setup_inputs(seed: int = 0) -> dict:
    splits = jax.random.split(jax.random.key(seed), 7)
    queries = bell_draw(splits[0], (BATCH, SEQ, WIDTH), 0.3, 1.75, ((0, 4), (1, 4), (2, 2)))
    keys_in = bell_draw(splits[1], (BATCH, SEQ, WIDTH), 0.3, 1.75, ((0, 4), (1, 4), (2, 2)))
    values = draw_values(jax.random.fold_in(splits[6], 71), 0)
    norm_gain = jnp.clip(1.0 + 0.15 * jax.random.normal(splits[3], (WIDTH,), jnp.float32), 0.25, 1.75)
    segment_ids = jax.vmap(lambda own: jnp.searchsorted(jnp.cumsum(uneven(own, 6, NBLK, NBLK // 2, 0)), jnp.arange(NBLK), side="right"))(jax.random.split(splits[4], BATCH)).reshape((BATCH, NBLK)).astype(jnp.int32)
    grad_out = draw_grad_out(jax.random.fold_in(splits[6], 71), 0)
    return {"queries": queries, "keys_in": keys_in, "values": values, "norm_gain": norm_gain, "segment_ids": segment_ids, "grad_out": grad_out}


def block_mask(seg_block):
    length = seg_block.shape[0]
    row_index = lax.broadcasted_iota(jnp.int32, (length, length), 0)
    col_index = lax.broadcasted_iota(jnp.int32, (length, length), 1)
    return jnp.logical_and(row_index >= col_index, seg_block[:, None] == seg_block[None, :])

def block_weights(q_block, k_block, visible):
    scores = jnp.einsum('thd,shd->hts', q_block.astype(jnp.float32), k_block.astype(jnp.float32))
    return jnp.where(visible[None], scores, 0.0).astype(jnp.bfloat16)

def forward_block(carried, block_in):
    kv_state, seg_prev = carried
    q_block, k_block, v_block, seg_block = block_in
    visible = block_mask(seg_block)
    weights = block_weights(q_block, k_block, visible)
    intra = jnp.einsum('hts,she->the', weights.astype(jnp.float32), v_block.astype(jnp.float32))
    state_bf = kv_state.astype(jnp.bfloat16)
    inter = jnp.einsum('thd,hde->the', q_block.astype(jnp.float32), state_bf.astype(jnp.float32))
    matches = (seg_block == seg_prev)[:, None, None]
    attended = intra + jnp.where(matches, inter, 0.0)
    last_seg = seg_block[-1]
    in_last = (seg_block == last_seg)[:, None, None]
    added = jnp.einsum('thd,the->hde', jnp.where(in_last, k_block.astype(jnp.float32), 0.0), v_block.astype(jnp.float32))
    new_state = jnp.where(seg_prev == last_seg, kv_state, 0.0) + added
    return ((new_state, last_seg), (attended, state_bf, seg_prev))

def backward_block(grad_state, block_in):
    q_block, k_block, v_block, seg_block, grad_block, state_bf, seg_prev = block_in
    visible = block_mask(seg_block)
    weights = block_weights(q_block, k_block, visible)
    q_f = q_block.astype(jnp.float32)
    k_f = k_block.astype(jnp.float32)
    v_f = v_block.astype(jnp.float32)
    grad_f = grad_block.astype(jnp.float32)
    grad_scores = jnp.einsum('the,she->hts', grad_f, v_f)
    grad_weights = jnp.where(visible[None], grad_scores, 0.0).astype(jnp.bfloat16).astype(jnp.float32)
    grad_bf = grad_state.astype(jnp.bfloat16).astype(jnp.float32)
    before = (seg_block == seg_prev)[:, None, None]
    after = (seg_block == seg_block[-1])[:, None, None]
    grad_q = jnp.einsum('hts,shd->thd', grad_weights, k_f) + jnp.where(before, jnp.einsum('the,hde->thd', grad_f, state_bf.astype(jnp.float32)), 0.0)
    grad_k = jnp.einsum('hts,thd->shd', grad_weights, q_f) + jnp.where(after, jnp.einsum('she,hde->shd', v_f, grad_bf), 0.0)
    grad_v = jnp.einsum('hts,the->she', weights.astype(jnp.float32), grad_f) + jnp.where(after, jnp.einsum('shd,hde->she', k_f, grad_bf), 0.0)
    added = jnp.einsum('thd,the->hde', jnp.where(before, q_f, 0.0), grad_f)
    new_grad = jnp.where(seg_prev == seg_block[-1], grad_state, 0.0) + added
    return (new_grad, (grad_q.astype(jnp.bfloat16), grad_k.astype(jnp.bfloat16), grad_v.astype(jnp.bfloat16)))

def to_blocks(array):
    return array.reshape(SEQ // BLK, BLK, HEADS, HD)

def sequence_forward(inputs):
    query_seq, key_seq, value_seq, seg_seq = inputs
    seg_blocks = seg_seq.reshape(SEQ // BLK, BLK)
    start = (jnp.zeros((HEADS, HD, HD), jnp.float32), seg_seq[0])
    final, outs_seq = lax.scan(forward_block, start, (to_blocks(query_seq), to_blocks(key_seq), to_blocks(value_seq), seg_blocks))
    attended, state_bf, seg_prev = outs_seq
    return (attended.reshape(SEQ, WIDTH), state_bf, seg_prev)

def sequence_backward(inputs):
    query_seq, key_seq, value_seq, seg_seq, grad_seq, state_bf, seg_prev = inputs
    seg_blocks = seg_seq.reshape(SEQ // BLK, BLK)
    start = jnp.zeros((HEADS, HD, HD), jnp.float32)
    final, grads = lax.scan(backward_block, start, (to_blocks(query_seq), to_blocks(key_seq), to_blocks(value_seq), seg_blocks, to_blocks(grad_seq), state_bf, seg_prev), reverse=True)
    return tuple((piece.reshape(SEQ, WIDTH) for piece in grads))

def reference(queries, keys_in, values, norm_gain, segment_ids, grad_out):
    seg_all = jnp.repeat(segment_ids, SEGB, axis=1).astype(jnp.int32)
    attended, state_bf, seg_prev = lax.map(sequence_forward, (queries, keys_in, values, seg_all))
    cotangent = grad_out.astype(jnp.float32)
    radius = jnp.sqrt(lax.optimization_barrier(jnp.mean(attended * attended, axis=2)) + 1e-06)
    normed = attended / radius[:, :, None]
    normed_out = (normed * norm_gain).astype(jnp.bfloat16)
    grad_gain = lax.optimization_barrier(jnp.sum(cotangent * normed, axis=(0, 1)))
    gained = cotangent * norm_gain
    inner = lax.optimization_barrier(jnp.sum(gained * attended, axis=2))
    grad_att = ((gained - attended * (inner / (WIDTH * radius * radius))[:, :, None]) / radius[:, :, None]).astype(jnp.bfloat16)
    grad_queries, grad_keys, grad_values = lax.map(sequence_backward, (queries, keys_in, values, seg_all, grad_att, state_bf, seg_prev))
    return (normed_out, grad_queries, grad_keys, grad_values, grad_gain)
```

```python
import functools

import jax
import jax.numpy as jnp
from jax import lax
from jax.experimental import pallas as pl
from jax.experimental.pallas import tpu as pltpu
from jax.sharding import PartitionSpec as P

HD = 128
BLK = 256
SEGB = 64
PARTS = 2
PER = BLK // SEGB
F32 = jnp.float32
BF16 = jnp.bfloat16
MESH = pl.DeviceIdType.MESH


def nn(a, b):
    return lax.dot_general(a, b, (((1,), (0,)), ((), ())), preferred_element_type=F32)


def nt(a, b):
    return lax.dot_general(a, b, (((1,), (1,)), ((), ())), preferred_element_type=F32)


def tn(a, b):
    return lax.dot_general(a, b, (((0,), (0,)), ((), ())), preferred_element_type=F32)


def flag(cond):
    return jnp.where(cond, 1.0, 0.0).astype(F32)


def spread(index, ids):
    out = jnp.full(index.shape, ids[-1], jnp.int32)
    for i in reversed(range(len(ids) - 1)):
        out = jnp.where(index < (i + 1) * SEGB, ids[i], out)
    return out


def kernel(
    nctx, ndp, heads, blocks, width,
    seg_hbm, gain_hbm, q_hbm, k_hbm, v_hbm, g_hbm,
    no_s, gq_s, gk_s, gv_s, gg_ref,
    seg_ref, gain_ref, qs, ks, vs, gs,
    att, gv_part, weights_t, visible, visible_t, mprev, mlast,
    local, state_bf, s_in, grad_local, g_in,
    sq_acc, in_acc, tile_out, tile_in, sums_out, sums_in,
    gg_part, gg_dp, gg_own, gg_down_out, gg_down_in, gg_up_out, gg_up_in, match_ref,
    in_sem, fs_sem, fr_sem, bs_sem, br_sem, ts_sem, tr_sem,
    xs_sem, xr_sem, ds_sem, dr_sem, cs_sem, cr_sem,
):
    ctx = lax.axis_index("context")
    ten = lax.axis_index("tensor")
    dp = lax.axis_index("dp")
    toks = blocks * BLK
    last = nctx - 1
    below = {"context": jnp.maximum(ctx - 1, 0)}
    above = {"context": jnp.minimum(ctx + 1, last)}
    inner = jnp.logical_and(ctx > 0, ctx < last)

    barrier = pltpu.get_barrier_semaphore()

    @pl.when(ctx > 0)
    def _():
        pl.semaphore_signal(barrier, inc=1, device_id=below, device_id_type=MESH)

    @pl.when(ctx < last)
    def _():
        pl.semaphore_signal(barrier, inc=1, device_id=above, device_id_type=MESH)

    pl.semaphore_signal(barrier, inc=1, device_id={"tensor": 1 - ten}, device_id_type=MESH)

    @pl.loop(1, ndp)
    def _(d):
        pl.semaphore_signal(
            barrier, inc=1, device_id={"dp": lax.rem(dp + d, ndp)}, device_id_type=MESH
        )

    seg_copy = pltpu.make_async_copy(seg_hbm, seg_ref, in_sem.at[4])
    gain_copy = pltpu.make_async_copy(gain_hbm, gain_ref, in_sem.at[5])
    seg_copy.start()
    gain_copy.start()

    ins = ((k_hbm, ks), (v_hbm, vs), (q_hbm, qs), (g_hbm, gs))

    for n, (src, dst) in enumerate(ins):
        @pl.loop(0, heads)
        def _(h):
            cols = pl.ds(pl.multiple_of(h * HD, HD), HD)
            pltpu.make_async_copy(src.at[0, :, cols], dst.at[h], in_sem.at[n]).start()

    def arrived(n):
        pltpu.make_async_copy(ins[n][1], ins[n][1], in_sem.at[n]).wait()

    seg_copy.wait()
    seg = [[seg_ref[0, j * PER + i] for i in range(PER)] for j in range(blocks)]
    lasts = [seg[j][-1] for j in range(blocks)]
    tile_out[...] = jnp.full((8, HD), lasts[-1], jnp.int32).astype(F32)
    rows_h = lax.broadcasted_iota(jnp.int32, (BLK, HD), 0)
    step = [flag(seg[0][0] == lasts[0])]
    for j in range(1, blocks):
        step.append(flag(lasts[j - 1] == lasts[j]))

    def rows_of(j):
        return pl.ds(j * BLK, BLK)

    for j in range(blocks):
        seg_h = spread(rows_h, seg[j])
        mlast[rows_of(j), :] = flag(seg_h == lasts[j]).astype(BF16)
        before = seg[0][0] if j == 0 else lasts[j - 1]
        mprev[rows_of(j), :] = flag(seg_h == before).astype(BF16)

    def tile_copy():
        return pltpu.make_async_remote_copy(
            tile_out, tile_in, ts_sem, tr_sem, device_id=above, device_id_type=MESH
        )

    def part(p):
        return pl.ds(p * (HD // PARTS), HD // PARTS)

    def fwd_copy(h, p):
        return pltpu.make_async_remote_copy(
            local.at[h, blocks - 1, part(p)], s_in.at[h, part(p)], fs_sem,
            fr_sem.at[h * PARTS + p], device_id=above, device_id_type=MESH,
        )

    def bwd_copy(h, p):
        return pltpu.make_async_remote_copy(
            grad_local.at[h, 0, part(p)], g_in.at[h, part(p)], bs_sem,
            br_sem.at[h * PARTS + p], device_id=below, device_id_type=MESH,
        )

    def local_sums(h):
        run = None
        for j in range(blocks):
            km = ks[h, rows_of(j), :] * mlast[rows_of(j), :]
            add = tn(km, vs[h, rows_of(j), :])
            run = add if run is None else run * step[j] + add
            local[h, j] = run

    def scores(h):
        for j in range(blocks):
            at = rows_of(j)
            w = (nt(qs[h, at, :], ks[h, at, :]) * visible[j]).astype(BF16)
            w_t = nt(ks[h, at, :], qs[h, at, :]) * visible_t[j]
            weights_t[h, j] = w_t.astype(BF16)
            att[h, at, :] = nn(w, vs[h, at, :])

    def first_send(h):
        @pl.when(jnp.logical_and(ctx == 0, ctx < last))
        def _():
            for p in range(PARTS):
                fwd_copy(h, p).start()

    arrived(0)
    arrived(1)
    local_sums(0)

    pl.semaphore_wait(
        barrier,
        ndp + jnp.where(ctx > 0, 1, 0) + jnp.where(ctx < last, 1, 0),
    )

    @pl.when(ctx < last)
    def _():
        tile_copy().start()

    first_send(0)

    @pl.when(ctx == 0)
    def _():
        s_in[...] = jnp.zeros_like(s_in)
        tile_in[...] = jnp.full((8, HD), -1.0, F32)

    @pl.when(ctx == last)
    def _():
        g_in[...] = jnp.zeros_like(g_in)

    rows = lax.broadcasted_iota(jnp.int32, (BLK, BLK), 0)
    cols = lax.broadcasted_iota(jnp.int32, (BLK, BLK), 1)
    for j in range(blocks):
        same = spread(rows, seg[j]) == spread(cols, seg[j])
        visible[j] = flag(jnp.logical_and(rows >= cols, same))
        visible_t[j] = flag(jnp.logical_and(cols >= rows, same))
    sq_acc[...] = jnp.zeros_like(sq_acc)
    in_acc[...] = jnp.zeros_like(in_acc)

    arrived(2)
    scores(0)
    gain_copy.wait()
    arrived(3)

    @pl.when(ctx > 0)
    def _():
        tile_copy().wait_recv()

    first = jnp.full((1, HD), seg[0][0], jnp.int32).astype(F32)
    match = flag(tile_in[0:1, :] == first)
    at0 = rows_of(0)
    mprev[at0, :] = (mprev[at0, :].astype(F32) * match).astype(BF16)
    reach = [match * step[0]]
    for j in range(1, blocks):
        reach.append(reach[-1] * step[j])

    def take_state(h, p):
        @pl.when(ctx > 0)
        def _():
            fwd_copy(h, p).wait_recv()

            @pl.when(ctx < last)
            def _():
                at = part(p)
                local[h, blocks - 1, at, :] = (
                    local[h, blocks - 1, at, :] + s_in[h, at, :] * reach[-1]
                )
                fwd_copy(h, p).start()

    def attend(h):
        gain = gain_ref[pl.ds(h, 1), :]
        came = s_in[h]
        for j in range(blocks):
            at = rows_of(j)
            state = came if j == 0 else local[h, j - 1] + came * reach[j - 1]
            state = state.astype(BF16)
            state_bf[h, j] = state
            a = att[h, at, :] + nn(qs[h, at, :] * mprev[at, :], state)
            att[h, at, :] = a
            sq_acc[at, :] += a * a
            in_acc[at, :] += a * (gs[h, at, :].astype(F32) * gain)

    @pl.loop(0, heads - 1)
    def _(h):
        take_state(h, 0)
        local_sums(h + 1)
        first_send(h + 1)
        scores(h + 1)
        for p in range(1, PARTS):
            take_state(h, p)
        attend(h)

    for p in range(PARTS):
        take_state(heads - 1, p)
    attend(heads - 1)

    groups = toks // HD
    eye = (
        lax.broadcasted_iota(jnp.int32, (HD, HD), 0) == lax.broadcasted_iota(jnp.int32, (HD, HD), 1)
    )
    for n, acc in ((0, sq_acc), (1, in_acc)):
        for i in range(groups):
            col = jnp.sum(acc[pl.ds(i * HD, HD), :], axis=1, keepdims=True)
            row = jnp.sum(
                jnp.where(eye, jnp.broadcast_to(col, (HD, HD)), 0.0), axis=0, keepdims=True
            )
            sums_out[n, pl.ds(i, 1), :] = row
    swap = pltpu.make_async_remote_copy(
        sums_out, sums_in, xs_sem, xr_sem, device_id={"tensor": 1 - ten}, device_id_type=MESH
    )
    swap.start()
    swap.wait()
    total_sq = sums_out[0] + sums_in[0]
    total_in = sums_out[1] + sums_in[1]
    radius = jnp.sqrt(total_sq / width + 1e-06)
    inv = 1.0 / radius
    sums_out[0] = inv
    sums_out[1] = total_in / (width * radius * radius) * inv
    for n, acc in ((0, sq_acc), (1, in_acc)):
        for i in range(groups):
            row = jnp.broadcast_to(sums_out[n, pl.ds(i, 1), :], (HD, HD))
            acc[pl.ds(i * HD, HD), :] = row.T

    keep = [match * step[0]] + step[1:]
    full = [None] * (blocks + 1)
    full[blocks] = 1.0
    for j in reversed(range(blocks)):
        full[j] = full[j + 1] * keep[j]

    @pl.loop(0, heads)
    def _(h):
        gain = gain_ref[pl.ds(h, 1), :]
        total = jnp.zeros((1, HD), F32)
        adds = []
        for j in range(blocks):
            at = rows_of(j)
            inv = sq_acc[at, :]
            a = att[h, at, :]
            g = gs[h, at, :].astype(F32)
            normed = a * inv
            no_s[h, at, :] = (normed * gain).astype(BF16)
            total = total + jnp.sum(g * normed, axis=0, keepdims=True)
            d = (g * gain * inv - a * in_acc[at, :]).astype(BF16)
            gs[h, at, :] = d
            adds.append(tn(qs[h, at, :] * mprev[at, :], d))
        gg_part[pl.ds(h, 1), :] = total
        run = None
        for j in reversed(range(blocks)):
            run = adds[j] if run is None else adds[j] + run * keep[j]
            grad_local[h, j] = run

        @pl.when(jnp.logical_and(ctx == last, ctx > 0))
        def _():
            for p in range(PARTS):
                bwd_copy(h, p).start()

    def dp_copy(to, slot):
        return pltpu.make_async_remote_copy(
            gg_part, gg_dp.at[slot], ds_sem, dr_sem.at[slot],
            device_id={"dp": to}, device_id_type=MESH,
        )

    gg_dp[dp] = gg_part[...]

    @pl.loop(1, ndp)
    def _(d):
        dp_copy(lax.rem(dp + d, ndp), dp).start()

    def down_copy():
        return pltpu.make_async_remote_copy(
            gg_down_out, gg_down_in, cs_sem.at[0], cr_sem.at[0], device_id=below, device_id_type=MESH
        )

    def up_copy():
        return pltpu.make_async_remote_copy(
            gg_up_out, gg_up_in, cs_sem.at[1], cr_sem.at[1], device_id=above, device_id_type=MESH
        )

    def take_grad(h, p):
        @pl.when(ctx < last)
        def _():
            bwd_copy(h, p).wait_recv()

            @pl.when(ctx > 0)
            def _():
                at = part(p)
                grad_local[h, 0, at, :] = grad_local[h, 0, at, :] + g_in[h, at, :] * full[0]
                bwd_copy(h, p).start()

    lag = jnp.clip(4 * (last - ctx) - 3, 0, heads)
    down_at = lag + jnp.clip(1 + last - ctx, 1, heads - 1)
    up_at = jnp.clip(3 * ctx, 1, heads + lag - 1)

    @pl.loop(0, heads + lag)
    def _(i):
        @pl.when(i >= lag)
        def _():
            take_grad(i - lag, 0)

        @pl.when(i < heads)
        def _():
            h = i
            for j in range(blocks):
                at = rows_of(j)
                d = gs[h, at, :]
                dw = (nt(d, vs[h, at, :]) * visible[j]).astype(BF16)
                gq = nn(dw, ks[h, at, :]) + nt(d * mprev[at, :], state_bf[h, j])
                gq_s[h, at, :] = gq.astype(BF16)
                dw_t = (nt(vs[h, at, :], d) * visible_t[j]).astype(BF16)
                att[h, at, :] = nn(dw_t, qs[h, at, :])
                gv_part[h, at, :] = nn(weights_t[h, j], d)

        @pl.when(i >= lag)
        def _():
            h = i - lag
            for p in range(1, PARTS):
                take_grad(h, p)
            came = g_in[h]
            for j in range(blocks):
                at = rows_of(j)
                grad = came if j == blocks - 1 else grad_local[h, j + 1] + came * full[j + 1]
                grad = grad.astype(BF16)
                ml = mlast[at, :]
                gk_s[h, at, :] = (att[h, at, :] + nt(vs[h, at, :] * ml, grad)).astype(BF16)
                gv_s[h, at, :] = (gv_part[h, at, :] + nn(ks[h, at, :] * ml, grad)).astype(BF16)

        @pl.when(i == 1)
        def _():
            @pl.loop(1, ndp)
            def _(d):
                peer = lax.rem(dp + d, ndp)
                dp_copy(peer, peer).wait_recv()

            own = gg_dp[0]
            for n in range(1, ndp):
                own = own + gg_dp[n]
            gg_own[...] = own

        @pl.when(jnp.logical_and(i == down_at, ctx > 0))
        def _():
            @pl.when(ctx < last)
            def _():
                down_copy().wait_recv()
                gg_down_out[...] = gg_own[...] + gg_down_in[...]

            @pl.when(ctx == last)
            def _():
                gg_down_out[...] = gg_own[...]

            down_copy().start()

        @pl.when(jnp.logical_and(i == up_at, ctx < last))
        def _():
            @pl.when(ctx > 0)
            def _():
                up_copy().wait_recv()
                gg_up_out[...] = gg_own[...] + gg_up_in[...]

            @pl.when(ctx == 0)
            def _():
                gg_up_out[...] = gg_own[...]

            up_copy().start()

    @pl.when(ctx == 0)
    def _():
        @pl.when(ctx < last)
        def _():
            down_copy().wait_recv()
            gg_ref[...] = gg_own[...] + gg_down_in[...]

        @pl.when(ctx == last)
        def _():
            gg_ref[...] = gg_own[...]

    @pl.when(inner)
    def _():
        gg_ref[...] = gg_up_out[...] + gg_down_in[...]

    @pl.when(jnp.logical_and(ctx > 0, ctx == last))
    def _():
        up_copy().wait_recv()
        gg_ref[...] = gg_up_in[...] + gg_own[...]

    pltpu.make_async_remote_copy(
        gg_dp.at[pl.ds(0, ndp - 1)], gg_dp.at[pl.ds(0, ndp - 1)], ds_sem, dr_sem.at[0],
        device_id={"dp": dp}, device_id_type=MESH,
    ).wait_send()

    @pl.when(ctx < last)
    def _():
        tile_copy().wait_send()
        up_copy().wait_send()
        pltpu.make_async_remote_copy(
            s_in, s_in, fs_sem, fr_sem.at[0], device_id=above, device_id_type=MESH
        ).wait_send()

    @pl.when(ctx > 0)
    def _():
        down_copy().wait_send()
        pltpu.make_async_remote_copy(
            g_in, g_in, bs_sem, br_sem.at[0], device_id=below, device_id_type=MESH
        ).wait_send()


def writer(heads, *refs):
    sems, gain_sem = refs[10:]
    small = pltpu.make_async_copy(refs[4], refs[9], gain_sem)
    small.start()

    def copy(n, h):
        cols = pl.ds(pl.multiple_of(h * HD, HD), HD)
        return pltpu.make_async_copy(refs[n].at[h], refs[5 + n].at[0, :, cols], sems.at[n, h])

    @pl.loop(0, heads)
    def _(h):
        for n in range(4):
            copy(n, h).start()

    @pl.loop(0, heads)
    def _(h):
        for n in range(4):
            copy(n, h).wait()

    small.wait()


def body(nctx, ndp, full_width, queries, keys_in, values, norm_gain, segment_ids, grad_out):
    toks, local_width = queries.shape[1:]
    heads = local_width // HD
    blocks = toks // BLK
    wide = jax.ShapeDtypeStruct(queries.shape, BF16)
    hbm = pl.BlockSpec(memory_space=pl.ANY)
    vmem = pl.BlockSpec(memory_space=pltpu.VMEM)
    per_head = pltpu.VMEM((heads, toks, HD), BF16)
    states = pltpu.VMEM((heads, blocks, HD, HD), F32)
    hops = pltpu.VMEM((heads, HD, HD), F32)
    rowish = pltpu.VMEM((toks, HD), F32)
    dma = pltpu.SemaphoreType.DMA
    groups = -(-(toks // HD) // 8) * 8
    sums = pltpu.VMEM((2, groups, HD), F32)
    tile = pltpu.VMEM((8, HD), F32)
    gains = pltpu.VMEM((heads, HD), F32)
    outs = pl.pallas_call(
        functools.partial(kernel, nctx, ndp, heads, blocks, full_width),
        out_shape=[pltpu.VMEM((heads, toks, HD), BF16)] * 4 + [pltpu.VMEM((heads, HD), F32)],
        in_specs=[hbm] * 6,
        out_specs=[vmem] * 5,
        scratch_shapes=[pltpu.SMEM(segment_ids.shape, jnp.int32), gains]
        + [per_head] * 4
        + [
            pltpu.VMEM((heads, toks, HD), F32),
            pltpu.VMEM((heads, toks, HD), F32),
            pltpu.VMEM((heads, blocks, BLK, BLK), BF16),
            pltpu.VMEM((blocks, BLK, BLK), F32),
            pltpu.VMEM((blocks, BLK, BLK), F32),
            pltpu.VMEM((toks, HD), BF16),
            pltpu.VMEM((toks, HD), BF16),
            states,
            pltpu.VMEM((heads, blocks, HD, HD), BF16),
            hops, states, hops,
            rowish, rowish,
            tile, tile, sums, sums,
            gains, pltpu.VMEM((ndp, heads, HD), F32),
            gains, gains, gains, gains, gains, tile,
            dma((6,)),
            dma, dma((heads * PARTS,)), dma, dma((heads * PARTS,)),
            dma, dma, dma, dma,
            dma, dma((ndp,)), dma((2,)), dma((2,)),
        ],
        compiler_params=pltpu.CompilerParams(
            collective_id=0, has_side_effects=True, vmem_limit_bytes=55 << 20
        ),
    )(segment_ids, norm_gain.reshape(heads, HD), queries, keys_in, values, grad_out)
    copies = pl.pallas_call(
        functools.partial(writer, heads),
        out_shape=[wide] * 4 + [jax.ShapeDtypeStruct((heads, HD), F32)],
        in_specs=[hbm] * 5,
        out_specs=[hbm] * 5,
        scratch_shapes=[dma((4, heads)), dma],
        compiler_params=pltpu.CompilerParams(vmem_limit_bytes=1 << 20),
    )(*outs)
    return (*copies[:4], copies[4].reshape(local_width))


def solution(mesh):
    wide = P("dp", "context", "tensor")
    in_specs = (wide, wide, wide, P("tensor"), P("dp", "context"), wide)
    out_specs = (wide, wide, wide, wide, P("tensor"))

    def run(queries, *rest):
        fn = functools.partial(
            body, mesh.shape["context"], mesh.shape["dp"], queries.shape[2]
        )
        return jax.shard_map(
            fn, mesh=mesh, in_specs=in_specs, out_specs=out_specs, check_vma=False
        )(queries, *rest)

    return run
```

```python
import functools

import jax
import jax.numpy as jnp
from jax import lax
from jax.experimental import pallas as pl
from jax.experimental.pallas import tpu as pltpu
from jax.sharding import PartitionSpec as P

HD = 128
BLK = 256
SEGB = 64
PARTS = 1
EARLY_F = 2
EARLY_B = 2
PER = BLK // SEGB
F32 = jnp.float32
BF16 = jnp.bfloat16
MESH = pl.DeviceIdType.MESH


def nn(a, b):
    return lax.dot_general(a, b, (((1,), (0,)), ((), ())), preferred_element_type=F32)


def nt(a, b):
    return lax.dot_general(a, b, (((1,), (1,)), ((), ())), preferred_element_type=F32)


def tn(a, b):
    return lax.dot_general(a, b, (((0,), (0,)), ((), ())), preferred_element_type=F32)


def flag(cond):
    return jnp.where(cond, 1.0, 0.0).astype(F32)


def spread(index, ids):
    out = jnp.full(index.shape, ids[-1], jnp.int32)
    for i in reversed(range(len(ids) - 1)):
        out = jnp.where(index < (i + 1) * SEGB, ids[i], out)
    return out


def kernel(
    nctx, ndp, heads, blocks, width, few_f, few_b,
    seg_hbm, gain_hbm, q_hbm, k_hbm, v_hbm, g_hbm,
    no_s, gq_s, gk_s, gv_s, gg_ref,
    seg_ref, gain_ref, qs, ks, vs, gs,
    att, gv_part, weights_t, visible, visible_t, mprev, mlast,
    local, state_bf, s_in, s_early, grad_local, g_in, g_early,
    sq_acc, in_acc, tile_out, tile_in, sums_out, sums_in,
    gg_part, gg_dp, gg_own, gg_down_out, gg_down_in, gg_up_out, gg_up_in, match_ref,
    in_sem, fs_sem, fr_sem, bs_sem, br_sem, es_sem, ef_sem, eb_sem, ts_sem, tr_sem,
    xs_sem, xr_sem, ds_sem, dr_sem, cs_sem, cr_sem,
):
    ctx = lax.axis_index("context")
    ten = lax.axis_index("tensor")
    dp = lax.axis_index("dp")
    toks = blocks * BLK
    last = nctx - 1
    below = {"context": jnp.maximum(ctx - 1, 0)}
    above = {"context": jnp.minimum(ctx + 1, last)}
    inner = jnp.logical_and(ctx > 0, ctx < last)
    many_f, many_b = heads - few_f, heads - few_b

    barrier = pltpu.get_barrier_semaphore()

    @pl.when(ctx > 0)
    def _():
        pl.semaphore_signal(barrier, inc=1, device_id=below, device_id_type=MESH)

    @pl.when(ctx < last)
    def _():
        pl.semaphore_signal(barrier, inc=1, device_id=above, device_id_type=MESH)

    pl.semaphore_signal(barrier, inc=1, device_id={"tensor": 1 - ten}, device_id_type=MESH)

    @pl.loop(1, ndp)
    def _(d):
        pl.semaphore_signal(
            barrier, inc=1, device_id={"dp": lax.rem(dp + d, ndp)}, device_id_type=MESH
        )

    seg_copy = pltpu.make_async_copy(seg_hbm, seg_ref, in_sem.at[4])
    gain_copy = pltpu.make_async_copy(gain_hbm, gain_ref, in_sem.at[5])
    seg_copy.start()
    gain_copy.start()

    ins = ((k_hbm, ks), (v_hbm, vs), (q_hbm, qs), (g_hbm, gs))

    def load(n, h, sem):
        src, dst = ins[n]
        cols = pl.ds(pl.multiple_of(h * HD, HD), HD)
        pltpu.make_async_copy(src.at[0, :, cols], dst.at[h], in_sem.at[sem]).start()

    for n in range(4):
        @pl.loop(0, heads)
        def _(h):
            load(n, h, n)

    def arrived(n):
        pltpu.make_async_copy(ins[n][1], ins[n][1], in_sem.at[n]).wait()

    seg_copy.wait()
    seg = [[seg_ref[0, j * PER + i] for i in range(PER)] for j in range(blocks)]
    lasts = [seg[j][-1] for j in range(blocks)]
    tile_out[...] = jnp.full((8, HD), lasts[-1], jnp.int32).astype(F32)
    rows_h = lax.broadcasted_iota(jnp.int32, (BLK, HD), 0)
    step = [flag(seg[0][0] == lasts[0])]
    for j in range(1, blocks):
        step.append(flag(lasts[j - 1] == lasts[j]))

    def rows_of(j):
        return pl.ds(j * BLK, BLK)

    for j in range(blocks):
        seg_h = spread(rows_h, seg[j])
        mlast[rows_of(j), :] = flag(seg_h == lasts[j]).astype(BF16)
        before = seg[0][0] if j == 0 else lasts[j - 1]
        mprev[rows_of(j), :] = flag(seg_h == before).astype(BF16)

    def tile_copy():
        return pltpu.make_async_remote_copy(
            tile_out, tile_in, ts_sem, tr_sem, device_id=above, device_id_type=MESH
        )

    def part(p):
        return pl.ds(p * (HD // PARTS), HD // PARTS)

    def fwd_copy(h, p, src=None):
        src = local.at[h, blocks - 1] if src is None else src
        return pltpu.make_async_remote_copy(
            src.at[part(p)], s_in.at[h, part(p)], fs_sem,
            fr_sem.at[h * PARTS + p], device_id=above, device_id_type=MESH,
        )

    def bwd_copy(h, p, src=None):
        src = grad_local.at[h, 0] if src is None else src
        return pltpu.make_async_remote_copy(
            src.at[part(p)], g_in.at[h, part(p)], bs_sem,
            br_sem.at[h * PARTS + p], device_id=below, device_id_type=MESH,
        )

    def early_f(x):
        return pltpu.make_async_remote_copy(
            local.at[many_f + x, blocks - 1], s_early.at[x], es_sem.at[0],
            ef_sem.at[x], device_id=above, device_id_type=MESH,
        )

    def early_b(x):
        return pltpu.make_async_remote_copy(
            grad_local.at[many_b + x, 0], g_early.at[x], es_sem.at[1],
            eb_sem.at[x], device_id=below, device_id_type=MESH,
        )

    def local_sums(h):
        run = None
        for j in range(blocks):
            km = ks[h, rows_of(j), :] * mlast[rows_of(j), :]
            add = tn(km, vs[h, rows_of(j), :])
            run = add if run is None else run * step[j] + add
            local[h, j] = run

    def scores(h, j):
        at = rows_of(j)
        w = (nt(qs[h, at, :], ks[h, at, :]) * visible[j]).astype(BF16)
        w_t = nt(ks[h, at, :], qs[h, at, :]) * visible_t[j]
        weights_t[h, j] = w_t.astype(BF16)
        att[h, at, :] = nn(w, vs[h, at, :])

    slots = [p * (blocks + 1) // PARTS for p in range(PARTS)]

    def interleave(take, piece):
        for n in range(blocks + 1):
            for p in range(PARTS):
                if slots[p] == n:
                    take(p)
            piece(n)

    def first_send(h):
        @pl.when(jnp.logical_and(ctx == 0, ctx < last))
        def _():
            for p in range(PARTS):
                fwd_copy(h, p).start()

    rows = lax.broadcasted_iota(jnp.int32, (BLK, BLK), 0)
    cols = lax.broadcasted_iota(jnp.int32, (BLK, BLK), 1)
    for j in range(blocks):
        same = spread(rows, seg[j]) == spread(cols, seg[j])
        visible[j] = flag(jnp.logical_and(rows >= cols, same))
        visible_t[j] = flag(jnp.logical_and(cols >= rows, same))
    sq_acc[...] = jnp.zeros_like(sq_acc)
    in_acc[...] = jnp.zeros_like(in_acc)

    @pl.when(ctx == 0)
    def _():
        s_in[...] = jnp.zeros_like(s_in)
        tile_in[...] = jnp.full((8, HD), -1.0, F32)

    @pl.when(ctx == last)
    def _():
        g_in[...] = jnp.zeros_like(g_in)

    arrived(0)
    arrived(1)
    local_sums(0)
    for x in range(few_f):
        local_sums(many_f + x)

    pl.semaphore_wait(
        barrier,
        ndp + jnp.where(ctx > 0, 1, 0) + jnp.where(ctx < last, 1, 0),
    )

    @pl.when(ctx < last)
    def _():
        tile_copy().start()

    first_send(0)

    if few_f:
        @pl.when(ctx == 1)
        def _():
            for x in range(few_f):
                early_f(x).start()

    @pl.loop(1, many_f)
    def _(h):
        local_sums(h)
        first_send(h)

    for x in range(few_f):
        first_send(many_f + x)

    arrived(2)
    turn_f = jnp.where(ctx == last, many_f, 0)
    for j in range(blocks):
        scores(lax.rem(turn_f, heads), j)
    gain_copy.wait()
    arrived(3)

    @pl.when(ctx > 0)
    def _():
        tile_copy().wait_recv()

    first = jnp.full((1, HD), seg[0][0], jnp.int32).astype(F32)
    match = flag(tile_in[0:1, :] == first)
    at0 = rows_of(0)
    mprev[at0, :] = (mprev[at0, :].astype(F32) * match).astype(BF16)
    reach = [match * step[0]]
    for j in range(1, blocks):
        reach.append(reach[-1] * step[j])

    if few_f:
        @pl.when(ctx == 2)
        def _():
            for x in range(few_f):
                h = many_f + x
                early_f(x).wait_recv()
                local[h, blocks - 1] = local[h, blocks - 1] + s_early[x] * reach[-1]
                for p in range(PARTS):
                    fwd_copy(h, p).start()

    def take_state(h, p):
        at = part(p)

        @pl.when(ctx > 0)
        def _():
            fwd_copy(h, p).wait_recv()

        @pl.when(jnp.logical_and(inner, h < many_f))
        def _():
            local[h, blocks - 1, at, :] = (
                local[h, blocks - 1, at, :] + s_in[h, at, :] * reach[-1]
            )
            fwd_copy(h, p).start()

        if few_f:
            @pl.when(jnp.logical_and(inner, h >= many_f))
            def _():
                x = h - many_f

                @pl.when(ctx == 1)
                def _():
                    s_early[x, at, :] = s_in[h, at, :] * reach[-1]
                    fwd_copy(h, p, s_early.at[x]).start()

                @pl.when(ctx == 2)
                def _():
                    s_in[h, at, :] = s_in[h, at, :] + s_early[x, at, :]

    def attend(h):
        gain = gain_ref[pl.ds(h, 1), :]
        came = s_in[h]
        for j in range(blocks):
            at = rows_of(j)
            state = came if j == 0 else local[h, j - 1] + came * reach[j - 1]
            state = state.astype(BF16)
            state_bf[h, j] = state
            a = att[h, at, :] + nn(qs[h, at, :] * mprev[at, :], state)
            att[h, at, :] = a
            sq_acc[at, :] += a * a
            in_acc[at, :] += a * (gs[h, at, :].astype(F32) * gain)

    @pl.loop(0, heads - 1)
    def _(i):
        h = lax.rem(i + turn_f, heads)
        after = lax.rem(h + 1, heads)

        def piece(n):
            if n < blocks:
                scores(after, n)
            else:
                attend(h)

        interleave(functools.partial(take_state, h), piece)

    final = lax.rem(heads - 1 + turn_f, heads)
    for p in range(PARTS):
        take_state(final, p)
    attend(final)

    groups = toks // HD
    eye = (
        lax.broadcasted_iota(jnp.int32, (HD, HD), 0) == lax.broadcasted_iota(jnp.int32, (HD, HD), 1)
    )
    for n, acc in ((0, sq_acc), (1, in_acc)):
        for i in range(groups):
            col = jnp.sum(acc[pl.ds(i * HD, HD), :], axis=1, keepdims=True)
            row = jnp.sum(
                jnp.where(eye, jnp.broadcast_to(col, (HD, HD)), 0.0), axis=0, keepdims=True
            )
            sums_out[n, pl.ds(i, 1), :] = row
    swap = pltpu.make_async_remote_copy(
        sums_out, sums_in, xs_sem, xr_sem, device_id={"tensor": 1 - ten}, device_id_type=MESH
    )
    swap.start()
    swap.wait()
    total_sq = sums_out[0] + sums_in[0]
    total_in = sums_out[1] + sums_in[1]
    radius = jnp.sqrt(total_sq / width + 1e-06)
    inv = 1.0 / radius
    sums_out[0] = inv
    sums_out[1] = total_in / (width * radius * radius) * inv
    for n, acc in ((0, sq_acc), (1, in_acc)):
        for i in range(groups):
            row = jnp.broadcast_to(sums_out[n, pl.ds(i, 1), :], (HD, HD))
            acc[pl.ds(i * HD, HD), :] = row.T

    keep = [match * step[0]] + step[1:]
    full = [None] * (blocks + 1)
    full[blocks] = 1.0
    for j in reversed(range(blocks)):
        full[j] = full[j + 1] * keep[j]

    first_rest = min(heads, 5)

    @pl.loop(0, heads)
    def _(i):
        h = lax.rem(i + jnp.where(ctx == 2, many_b, 0), heads)
        gain = gain_ref[pl.ds(h, 1), :]
        total = jnp.zeros((1, HD), F32)
        adds = []
        for j in range(blocks):
            at = rows_of(j)
            inv = sq_acc[at, :]
            a = att[h, at, :]
            g = gs[h, at, :].astype(F32)
            normed = a * inv
            no_s[h, at, :] = (normed * gain).astype(BF16)
            total = total + jnp.sum(g * normed, axis=0, keepdims=True)
            d = (g * gain * inv - a * in_acc[at, :]).astype(BF16)
            gs[h, at, :] = d
            adds.append(tn(qs[h, at, :] * mprev[at, :], d))
        gg_part[pl.ds(h, 1), :] = total
        run = None
        for j in reversed(range(blocks)):
            run = adds[j] if run is None else adds[j] + run * keep[j]
            grad_local[h, j] = run

        @pl.when(jnp.logical_and(ctx == last, jnp.logical_and(ctx > 0, h < first_rest)))
        def _():
            for p in range(PARTS):
                bwd_copy(h, p).start()

        if few_b:
            @pl.when(jnp.logical_and(ctx == 2, h >= many_b))
            def _():
                early_b(h - many_b).start()

    def dp_copy(to, slot):
        return pltpu.make_async_remote_copy(
            gg_part, gg_dp.at[slot], ds_sem, dr_sem.at[slot],
            device_id={"dp": to}, device_id_type=MESH,
        )

    gg_dp[dp] = gg_part[...]

    @pl.loop(1, ndp)
    def _(d):
        dp_copy(lax.rem(dp + d, ndp), dp).start()

    def down_copy():
        return pltpu.make_async_remote_copy(
            gg_down_out, gg_down_in, cs_sem.at[0], cr_sem.at[0], device_id=below, device_id_type=MESH
        )

    def up_copy():
        return pltpu.make_async_remote_copy(
            gg_up_out, gg_up_in, cs_sem.at[1], cr_sem.at[1], device_id=above, device_id_type=MESH
        )

    def take_grad(h, p):
        at = part(p)

        @pl.when(ctx < last)
        def _():
            bwd_copy(h, p).wait_recv()

        @pl.when(jnp.logical_and(inner, h < many_b))
        def _():
            grad_local[h, 0, at, :] = grad_local[h, 0, at, :] + g_in[h, at, :] * full[0]
            bwd_copy(h, p).start()

        if few_b:
            @pl.when(jnp.logical_and(inner, h >= many_b))
            def _():
                x = h - many_b

                @pl.when(ctx == 2)
                def _():
                    g_early[x, at, :] = g_in[h, at, :] * full[0]
                    bwd_copy(h, p, g_early.at[x]).start()

                @pl.when(ctx == 1)
                def _():
                    g_in[h, at, :] = g_in[h, at, :] + g_early[x, at, :]

    def send_down():
        @pl.when(inner)
        def _():
            down_copy().wait_recv()
            gg_down_out[...] = gg_own[...] + gg_down_in[...]

        @pl.when(jnp.logical_and(ctx > 0, ctx == last))
        def _():
            gg_down_out[...] = gg_own[...]

        @pl.when(ctx > 0)
        def _():
            down_copy().start()

        @pl.when(jnp.logical_and(ctx > 0, ctx == last))
        def _():
            for h in range(first_rest, heads):
                for p in range(PARTS):
                    bwd_copy(h, p).start()

    lag = jnp.clip(6 * (last - ctx) - 5, 0, heads)
    turn_b = jnp.where(ctx == 0, many_b, 0)
    down_at = lag + jnp.clip(3 + last - ctx, 3, heads - 1)
    up_at = jnp.clip(3 * ctx, 3, heads + lag - 1)

    @pl.loop(0, heads + lag)
    def _(i):
        done = lax.rem(jnp.maximum(i - lag, 0) + turn_b, heads)

        if few_b:
            @pl.when(jnp.logical_and(ctx == 1, i == lag))
            def _():
                for x in range(few_b):
                    h = many_b + x
                    early_b(x).wait_recv()
                    grad_local[h, 0] = grad_local[h, 0] + g_early[x] * full[0]
                    for p in range(PARTS):
                        bwd_copy(h, p).start()

        @pl.when(i == 3)
        def _():
            @pl.loop(1, ndp)
            def _(d):
                peer = lax.rem(dp + d, ndp)
                dp_copy(peer, peer).wait_recv()

            own = gg_dp[0]
            for n in range(1, ndp):
                own = own + gg_dp[n]
            gg_own[...] = own

        def take(p):
            @pl.when(i >= lag)
            def _():
                take_grad(done, p)

        def intra(j):
            @pl.when(i < heads)
            def _():
                h = i
                at = rows_of(j)
                d = gs[h, at, :]
                dw = (nt(d, vs[h, at, :]) * visible[j]).astype(BF16)
                gq = nn(dw, ks[h, at, :]) + nt(d * mprev[at, :], state_bf[h, j])
                gq_s[h, at, :] = gq.astype(BF16)
                dw_t = (nt(vs[h, at, :], d) * visible_t[j]).astype(BF16)
                att[h, at, :] = nn(dw_t, qs[h, at, :])
                gv_part[h, at, :] = nn(weights_t[h, j], d)

        def finish():
            h = done
            came = g_in[h]
            for j in range(blocks):
                at = rows_of(j)
                grad = came if j == blocks - 1 else grad_local[h, j + 1] + came * full[j + 1]
                grad = grad.astype(BF16)
                ml = mlast[at, :]
                gk_s[h, at, :] = (att[h, at, :] + nt(vs[h, at, :] * ml, grad)).astype(BF16)
                gv_s[h, at, :] = (gv_part[h, at, :] + nn(ks[h, at, :] * ml, grad)).astype(BF16)

        def piece(n):
            if n < blocks:
                intra(n)
            else:
                pl.when(i == down_at)(send_down)
                pl.when(i >= lag)(finish)

        interleave(take, piece)

        @pl.when(jnp.logical_and(i == up_at, ctx < last))
        def _():
            @pl.when(ctx > 0)
            def _():
                up_copy().wait_recv()
                gg_up_out[...] = gg_own[...] + gg_up_in[...]

            @pl.when(ctx == 0)
            def _():
                gg_up_out[...] = gg_own[...]

            up_copy().start()

    @pl.when(ctx == 0)
    def _():
        @pl.when(ctx < last)
        def _():
            down_copy().wait_recv()
            gg_ref[...] = gg_own[...] + gg_down_in[...]

        @pl.when(ctx == last)
        def _():
            gg_ref[...] = gg_own[...]

    @pl.when(inner)
    def _():
        gg_ref[...] = gg_up_out[...] + gg_down_in[...]

    @pl.when(jnp.logical_and(ctx > 0, ctx == last))
    def _():
        up_copy().wait_recv()
        gg_ref[...] = gg_up_in[...] + gg_own[...]

    pltpu.make_async_remote_copy(
        gg_dp.at[pl.ds(0, ndp - 1)], gg_dp.at[pl.ds(0, ndp - 1)], ds_sem, dr_sem.at[0],
        device_id={"dp": dp}, device_id_type=MESH,
    ).wait_send()

    @pl.when(ctx < last)
    def _():
        tile_copy().wait_send()
        up_copy().wait_send()
        pltpu.make_async_remote_copy(
            s_in, s_in, fs_sem, fr_sem.at[0], device_id=above, device_id_type=MESH
        ).wait_send()

    if few_f:
        @pl.when(ctx == 1)
        def _():
            pltpu.make_async_remote_copy(
                s_early, s_early, es_sem.at[0], ef_sem.at[0], device_id=above, device_id_type=MESH
            ).wait_send()

    if few_b:
        @pl.when(ctx == 2)
        def _():
            pltpu.make_async_remote_copy(
                g_early, g_early, es_sem.at[1], eb_sem.at[0], device_id=below, device_id_type=MESH
            ).wait_send()

    @pl.when(ctx > 0)
    def _():
        down_copy().wait_send()
        pltpu.make_async_remote_copy(
            g_in, g_in, bs_sem, br_sem.at[0], device_id=below, device_id_type=MESH
        ).wait_send()


def writer(heads, *refs):
    sems, gain_sem = refs[10:]
    small = pltpu.make_async_copy(refs[4], refs[9], gain_sem)
    small.start()

    def copy(n, h):
        cols = pl.ds(pl.multiple_of(h * HD, HD), HD)
        return pltpu.make_async_copy(refs[n].at[h], refs[5 + n].at[0, :, cols], sems.at[n, h])

    @pl.loop(0, heads)
    def _(h):
        for n in range(4):
            copy(n, h).start()

    @pl.loop(0, heads)
    def _(h):
        for n in range(4):
            copy(n, h).wait()

    small.wait()


def body(nctx, ndp, full_width, queries, keys_in, values, norm_gain, segment_ids, grad_out):
    toks, local_width = queries.shape[1:]
    heads = local_width // HD
    blocks = toks // BLK
    wide = jax.ShapeDtypeStruct(queries.shape, BF16)
    hbm = pl.BlockSpec(memory_space=pl.ANY)
    vmem = pl.BlockSpec(memory_space=pltpu.VMEM)
    per_head = pltpu.VMEM((heads, toks, HD), BF16)
    states = pltpu.VMEM((heads, blocks, HD, HD), F32)
    hops = pltpu.VMEM((heads, HD, HD), F32)
    ids = segment_ids.shape[1]
    short = nctx == 4 and 2 * ids + 2 > nctx * ids // 2
    few_f, few_b = (EARLY_F, EARLY_B) if short else (0, 0)

    def early(few):
        return pltpu.VMEM((max(few, 1), HD, HD), F32)

    rowish = pltpu.VMEM((toks, HD), F32)
    dma = pltpu.SemaphoreType.DMA
    groups = -(-(toks // HD) // 8) * 8
    sums = pltpu.VMEM((2, groups, HD), F32)
    tile = pltpu.VMEM((8, HD), F32)
    gains = pltpu.VMEM((heads, HD), F32)
    outs = pl.pallas_call(
        functools.partial(kernel, nctx, ndp, heads, blocks, full_width, few_f, few_b),
        out_shape=[pltpu.VMEM((heads, toks, HD), BF16)] * 4 + [pltpu.VMEM((heads, HD), F32)],
        in_specs=[hbm] * 6,
        out_specs=[vmem] * 5,
        scratch_shapes=[pltpu.SMEM(segment_ids.shape, jnp.int32), gains]
        + [per_head] * 4
        + [
            pltpu.VMEM((heads, toks, HD), F32),
            pltpu.VMEM((heads, toks, HD), F32),
            pltpu.VMEM((heads, blocks, BLK, BLK), BF16),
            pltpu.VMEM((blocks, BLK, BLK), F32),
            pltpu.VMEM((blocks, BLK, BLK), F32),
            pltpu.VMEM((toks, HD), BF16),
            pltpu.VMEM((toks, HD), BF16),
            states,
            pltpu.VMEM((heads, blocks, HD, HD), BF16),
            hops, early(few_f), states, hops, early(few_b),
            rowish, rowish,
            tile, tile, sums, sums,
            gains, pltpu.VMEM((ndp, heads, HD), F32),
            gains, gains, gains, gains, gains, tile,
            dma((6,)),
            dma, dma((heads * PARTS,)), dma, dma((heads * PARTS,)),
            dma((2,)), dma((max(few_f, 1),)), dma((max(few_b, 1),)),
            dma, dma, dma, dma,
            dma, dma((ndp,)), dma((2,)), dma((2,)),
        ],
        compiler_params=pltpu.CompilerParams(
            collective_id=0, has_side_effects=True, vmem_limit_bytes=55 << 20
        ),
    )(segment_ids, norm_gain.reshape(heads, HD), queries, keys_in, values, grad_out)
    copies = pl.pallas_call(
        functools.partial(writer, heads),
        out_shape=[wide] * 4 + [jax.ShapeDtypeStruct((heads, HD), F32)],
        in_specs=[hbm] * 5,
        out_specs=[hbm] * 5,
        scratch_shapes=[dma((4, heads)), dma],
        compiler_params=pltpu.CompilerParams(vmem_limit_bytes=1 << 20),
    )(*outs)
    return (*copies[:4], copies[4].reshape(local_width))


def solution(mesh):
    wide = P("dp", "context", "tensor")
    in_specs = (wide, wide, wide, P("tensor"), P("dp", "context"), wide)
    out_specs = (wide, wide, wide, wide, P("tensor"))

    def run(queries, *rest):
        fn = functools.partial(
            body, mesh.shape["context"], mesh.shape["dp"], queries.shape[2]
        )
        return jax.shard_map(
            fn, mesh=mesh, in_specs=in_specs, out_specs=out_specs, check_vma=False
        )(queries, *rest)

    return run
```

```python
import functools

import jax
import jax.numpy as jnp
from jax import lax
from jax.experimental import pallas as pl
from jax.experimental.pallas import tpu as pltpu
from jax.sharding import PartitionSpec as P

HD = 128
BLK = 256
SEGB = 64
PARTS_F = 2
PARTS_B = 1
EARLY_F = 2
EARLY_B = 3
PER = BLK // SEGB
F32 = jnp.float32
BF16 = jnp.bfloat16
MESH = pl.DeviceIdType.MESH


def nn(a, b):
    return lax.dot_general(a, b, (((1,), (0,)), ((), ())), preferred_element_type=F32)


def nt(a, b):
    return lax.dot_general(a, b, (((1,), (1,)), ((), ())), preferred_element_type=F32)


def tn(a, b):
    return lax.dot_general(a, b, (((0,), (0,)), ((), ())), preferred_element_type=F32)


def flag(cond):
    return jnp.where(cond, 1.0, 0.0).astype(F32)


def spread(index, ids):
    out = jnp.full(index.shape, ids[-1], jnp.int32)
    for i in reversed(range(len(ids) - 1)):
        out = jnp.where(index < (i + 1) * SEGB, ids[i], out)
    return out


def kernel(
    nctx, ndp, heads, blocks, width, few_f, few_b,
    seg_hbm, gain_hbm, q_hbm, k_hbm, v_hbm, g_hbm,
    no_s, gq_s, gk_s, gv_s, gg_ref,
    seg_ref, gain_ref, qs, ks, vs, gs,
    att, gv_part, weights_t, visible, visible_t, mprev, mlast,
    local, state_bf, s_in, s_early, grad_local, g_in, g_early,
    sq_acc, in_acc, tile_out, tile_in, sums_out, sums_in,
    gg_part, gg_dp, gg_own, gg_down_out, gg_down_in, gg_up_out, gg_up_in, match_ref,
    in_sem, fs_sem, fr_sem, bs_sem, br_sem, es_sem, ef_sem, eb_sem, ts_sem, tr_sem,
    xs_sem, xr_sem, ds_sem, dr_sem, cs_sem, cr_sem,
):
    ctx = lax.axis_index("context")
    ten = lax.axis_index("tensor")
    dp = lax.axis_index("dp")
    toks = blocks * BLK
    last = nctx - 1
    below = {"context": jnp.maximum(ctx - 1, 0)}
    above = {"context": jnp.minimum(ctx + 1, last)}
    inner = jnp.logical_and(ctx > 0, ctx < last)
    many_f, many_b = heads - few_f, heads - few_b

    barrier = pltpu.get_barrier_semaphore()

    @pl.when(ctx > 0)
    def _():
        pl.semaphore_signal(barrier, inc=1, device_id=below, device_id_type=MESH)

    @pl.when(ctx < last)
    def _():
        pl.semaphore_signal(barrier, inc=1, device_id=above, device_id_type=MESH)

    pl.semaphore_signal(barrier, inc=1, device_id={"tensor": 1 - ten}, device_id_type=MESH)

    @pl.loop(1, ndp)
    def _(d):
        pl.semaphore_signal(
            barrier, inc=1, device_id={"dp": lax.rem(dp + d, ndp)}, device_id_type=MESH
        )

    seg_copy = pltpu.make_async_copy(seg_hbm, seg_ref, in_sem.at[4])
    gain_copy = pltpu.make_async_copy(gain_hbm, gain_ref, in_sem.at[5])
    seg_copy.start()
    gain_copy.start()

    ins = ((k_hbm, ks), (v_hbm, vs), (q_hbm, qs), (g_hbm, gs))

    def load(n, h, sem):
        src, dst = ins[n]
        cols = pl.ds(pl.multiple_of(h * HD, HD), HD)
        pltpu.make_async_copy(src.at[0, :, cols], dst.at[h], in_sem.at[sem]).start()

    for n in range(4):
        @pl.loop(0, heads)
        def _(h):
            load(n, h, n)

    def arrived(n):
        pltpu.make_async_copy(ins[n][1], ins[n][1], in_sem.at[n]).wait()

    seg_copy.wait()
    seg = [[seg_ref[0, j * PER + i] for i in range(PER)] for j in range(blocks)]
    lasts = [seg[j][-1] for j in range(blocks)]
    tile_out[...] = jnp.full((8, HD), lasts[-1], jnp.int32).astype(F32)
    rows_h = lax.broadcasted_iota(jnp.int32, (BLK, HD), 0)
    step = [flag(seg[0][0] == lasts[0])]
    for j in range(1, blocks):
        step.append(flag(lasts[j - 1] == lasts[j]))

    def rows_of(j):
        return pl.ds(j * BLK, BLK)

    for j in range(blocks):
        seg_h = spread(rows_h, seg[j])
        mlast[rows_of(j), :] = flag(seg_h == lasts[j]).astype(BF16)
        before = seg[0][0] if j == 0 else lasts[j - 1]
        mprev[rows_of(j), :] = flag(seg_h == before).astype(BF16)

    def tile_copy():
        return pltpu.make_async_remote_copy(
            tile_out, tile_in, ts_sem, tr_sem, device_id=above, device_id_type=MESH
        )

    def part(p, parts):
        return pl.ds(p * (HD // parts), HD // parts)

    def fwd_copy(h, p, src=None):
        src = local.at[h, blocks - 1] if src is None else src
        return pltpu.make_async_remote_copy(
            src.at[part(p, PARTS_F)], s_in.at[h, part(p, PARTS_F)], fs_sem,
            fr_sem.at[h * PARTS_F + p], device_id=above, device_id_type=MESH,
        )

    def bwd_copy(h, p, src=None):
        src = grad_local.at[h, 0] if src is None else src
        return pltpu.make_async_remote_copy(
            src.at[part(p, PARTS_B)], g_in.at[h, part(p, PARTS_B)], bs_sem,
            br_sem.at[h * PARTS_B + p], device_id=below, device_id_type=MESH,
        )

    def early_f(x):
        return pltpu.make_async_remote_copy(
            local.at[many_f + x, blocks - 1], s_early.at[x], es_sem.at[0],
            ef_sem.at[x], device_id=above, device_id_type=MESH,
        )

    def early_b(x):
        return pltpu.make_async_remote_copy(
            grad_local.at[many_b + x, 0], g_early.at[x], es_sem.at[1],
            eb_sem.at[x], device_id=below, device_id_type=MESH,
        )

    def local_sums(h):
        run = None
        for j in range(blocks):
            km = ks[h, rows_of(j), :] * mlast[rows_of(j), :]
            add = tn(km, vs[h, rows_of(j), :])
            run = add if run is None else run * step[j] + add
            local[h, j] = run

    def scores(h, j):
        at = rows_of(j)
        w = (nt(qs[h, at, :], ks[h, at, :]) * visible[j]).astype(BF16)
        w_t = nt(ks[h, at, :], qs[h, at, :]) * visible_t[j]
        weights_t[h, j] = w_t.astype(BF16)
        att[h, at, :] = nn(w, vs[h, at, :])

    def interleave(parts, take, piece):
        for n in range(blocks + 1):
            for p in range(parts):
                if p * (blocks + 1) // parts == n:
                    take(p)
            piece(n)

    def first_send(h):
        @pl.when(jnp.logical_and(ctx == 0, ctx < last))
        def _():
            for p in range(PARTS_F):
                fwd_copy(h, p).start()

    rows = lax.broadcasted_iota(jnp.int32, (BLK, BLK), 0)
    cols = lax.broadcasted_iota(jnp.int32, (BLK, BLK), 1)
    for j in range(blocks):
        same = spread(rows, seg[j]) == spread(cols, seg[j])
        visible[j] = flag(jnp.logical_and(rows >= cols, same))
        visible_t[j] = flag(jnp.logical_and(cols >= rows, same))
    sq_acc[...] = jnp.zeros_like(sq_acc)
    in_acc[...] = jnp.zeros_like(in_acc)

    @pl.when(ctx == 0)
    def _():
        s_in[...] = jnp.zeros_like(s_in)
        tile_in[...] = jnp.full((8, HD), -1.0, F32)

    @pl.when(ctx == last)
    def _():
        g_in[...] = jnp.zeros_like(g_in)

    arrived(0)
    arrived(1)
    local_sums(0)
    for x in range(few_f):
        local_sums(many_f + x)

    pl.semaphore_wait(
        barrier,
        ndp + jnp.where(ctx > 0, 1, 0) + jnp.where(ctx < last, 1, 0),
    )

    @pl.when(ctx < last)
    def _():
        tile_copy().start()

    first_send(0)

    if few_f:
        @pl.when(ctx == 1)
        def _():
            for x in range(few_f):
                early_f(x).start()

    @pl.loop(1, many_f)
    def _(h):
        local_sums(h)
        first_send(h)

    for x in range(few_f):
        first_send(many_f + x)

    arrived(2)
    turn_f = jnp.where(ctx == last, many_f, 0)
    for j in range(blocks):
        scores(lax.rem(turn_f, heads), j)
    gain_copy.wait()
    arrived(3)

    @pl.when(ctx > 0)
    def _():
        tile_copy().wait_recv()

    first = jnp.full((1, HD), seg[0][0], jnp.int32).astype(F32)
    match = flag(tile_in[0:1, :] == first)
    at0 = rows_of(0)
    mprev[at0, :] = (mprev[at0, :].astype(F32) * match).astype(BF16)
    reach = [match * step[0]]
    for j in range(1, blocks):
        reach.append(reach[-1] * step[j])

    if few_f:
        @pl.when(ctx == 2)
        def _():
            for x in range(few_f):
                h = many_f + x
                early_f(x).wait_recv()
                local[h, blocks - 1] = local[h, blocks - 1] + s_early[x] * reach[-1]
                for p in range(PARTS_F):
                    fwd_copy(h, p).start()

    def take_state(h, p):
        at = part(p, PARTS_F)

        @pl.when(ctx > 0)
        def _():
            fwd_copy(h, p).wait_recv()

        @pl.when(jnp.logical_and(inner, h < many_f))
        def _():
            local[h, blocks - 1, at, :] = (
                local[h, blocks - 1, at, :] + s_in[h, at, :] * reach[-1]
            )
            fwd_copy(h, p).start()

        if few_f:
            @pl.when(jnp.logical_and(inner, h >= many_f))
            def _():
                x = h - many_f

                @pl.when(ctx == 1)
                def _():
                    s_early[x, at, :] = s_in[h, at, :] * reach[-1]
                    fwd_copy(h, p, s_early.at[x]).start()

                @pl.when(ctx == 2)
                def _():
                    s_in[h, at, :] = s_in[h, at, :] + s_early[x, at, :]

    def attend(h):
        gain = gain_ref[pl.ds(h, 1), :]
        came = s_in[h]
        for j in range(blocks):
            at = rows_of(j)
            state = came if j == 0 else local[h, j - 1] + came * reach[j - 1]
            state = state.astype(BF16)
            state_bf[h, j] = state
            a = att[h, at, :] + nn(qs[h, at, :] * mprev[at, :], state)
            att[h, at, :] = a
            sq_acc[at, :] += a * a
            in_acc[at, :] += a * (gs[h, at, :].astype(F32) * gain)

    @pl.loop(0, heads - 1)
    def _(i):
        h = lax.rem(i + turn_f, heads)
        after = lax.rem(h + 1, heads)

        def piece(n):
            if n < blocks:
                scores(after, n)
            else:
                attend(h)

        interleave(PARTS_F, functools.partial(take_state, h), piece)

    final = lax.rem(heads - 1 + turn_f, heads)
    for p in range(PARTS_F):
        take_state(final, p)
    attend(final)

    ones = jnp.ones((16, HD), BF16)
    for n, acc in ((0, sq_acc), (1, in_acc)):
        whole = acc[...]
        high = whole.astype(BF16)
        low = (whole - high.astype(F32)).astype(BF16)
        sums_out[n] = (nt(ones, high) + nt(ones, low))[0:8, :]
    swap = pltpu.make_async_remote_copy(
        sums_out, sums_in, xs_sem, xr_sem, device_id={"tensor": 1 - ten}, device_id_type=MESH
    )
    swap.start()
    swap.wait()
    total_sq = sums_out[0] + sums_in[0]
    total_in = sums_out[1] + sums_in[1]
    radius = jnp.sqrt(total_sq / width + 1e-06)
    inv = 1.0 / radius
    level = lax.broadcasted_iota(jnp.int32, (8, toks), 0)
    for acc, row in ((sq_acc, inv), (in_acc, total_in / (width * radius * radius) * inv)):
        high = row.astype(BF16).astype(F32)
        low = row - high
        middle = low.astype(BF16).astype(F32)
        split = jnp.where(level == 0, high, jnp.where(level == 1, middle, low - middle))
        split = jnp.where(level < 3, split, 0.0)
        split = jnp.concatenate([split, jnp.zeros_like(split)], axis=0).astype(BF16)
        acc[...] = tn(split, ones)

    keep = [match * step[0]] + step[1:]
    full = [None] * (blocks + 1)
    full[blocks] = 1.0
    for j in reversed(range(blocks)):
        full[j] = full[j + 1] * keep[j]

    first_rest = min(many_b, 5)

    @pl.loop(0, heads)
    def _(i):
        h = lax.rem(i + jnp.where(ctx == 2, many_b, 0), heads)
        gain = gain_ref[pl.ds(h, 1), :]
        total = jnp.zeros((1, HD), F32)
        adds = []
        for j in range(blocks):
            at = rows_of(j)
            inv = sq_acc[at, :]
            a = att[h, at, :]
            g = gs[h, at, :].astype(F32)
            normed = a * inv
            no_s[h, at, :] = (normed * gain).astype(BF16)
            total = total + jnp.sum(g * normed, axis=0, keepdims=True)
            d = (g * gain * inv - a * in_acc[at, :]).astype(BF16)
            gs[h, at, :] = d
            adds.append(tn(qs[h, at, :] * mprev[at, :], d))
        gg_part[pl.ds(h, 1), :] = total
        run = None
        for j in reversed(range(blocks)):
            run = adds[j] if run is None else adds[j] + run * keep[j]
            grad_local[h, j] = run

        @pl.when(jnp.logical_and(ctx == last, jnp.logical_and(ctx > 0, h < first_rest)))
        def _():
            for p in range(PARTS_B):
                bwd_copy(h, p).start()

        if few_b:
            @pl.when(jnp.logical_and(ctx == 2, h >= many_b))
            def _():
                early_b(h - many_b).start()

    def dp_copy(to, slot):
        return pltpu.make_async_remote_copy(
            gg_part, gg_dp.at[slot], ds_sem, dr_sem.at[slot],
            device_id={"dp": to}, device_id_type=MESH,
        )

    gg_dp[dp] = gg_part[...]

    @pl.loop(1, ndp)
    def _(d):
        dp_copy(lax.rem(dp + d, ndp), dp).start()

    def down_copy():
        return pltpu.make_async_remote_copy(
            gg_down_out, gg_down_in, cs_sem.at[0], cr_sem.at[0], device_id=below, device_id_type=MESH
        )

    def up_copy():
        return pltpu.make_async_remote_copy(
            gg_up_out, gg_up_in, cs_sem.at[1], cr_sem.at[1], device_id=above, device_id_type=MESH
        )

    def take_grad(h, p):
        at = part(p, PARTS_B)

        @pl.when(ctx < last)
        def _():
            bwd_copy(h, p).wait_recv()

        @pl.when(jnp.logical_and(inner, h < many_b))
        def _():
            grad_local[h, 0, at, :] = grad_local[h, 0, at, :] + g_in[h, at, :] * full[0]
            bwd_copy(h, p).start()

        if few_b:
            @pl.when(jnp.logical_and(inner, h >= many_b))
            def _():
                x = h - many_b

                @pl.when(ctx == 2)
                def _():
                    g_early[x, at, :] = g_in[h, at, :] * full[0]
                    bwd_copy(h, p, g_early.at[x]).start()

                @pl.when(ctx == 1)
                def _():
                    g_in[h, at, :] = g_in[h, at, :] + g_early[x, at, :]

    def send_down():
        @pl.when(inner)
        def _():
            down_copy().wait_recv()
            gg_down_out[...] = gg_own[...] + gg_down_in[...]

        @pl.when(jnp.logical_and(ctx > 0, ctx == last))
        def _():
            gg_down_out[...] = gg_own[...]

        @pl.when(ctx > 0)
        def _():
            down_copy().start()

        @pl.when(jnp.logical_and(ctx > 0, ctx == last))
        def _():
            for h in range(first_rest, heads):
                for p in range(PARTS_B):
                    bwd_copy(h, p).start()

    lag = jnp.where(ctx == 0, heads, jnp.clip(2 * (last - ctx) - 1, 0, heads))
    turn_b = jnp.where(ctx == 0, many_b, 0)
    down_at = lag + jnp.where(ctx == last, min(3, heads - 1), first_rest - 1)
    up_at = jnp.clip(3 * ctx, 3, heads + lag - 1)

    @pl.loop(0, heads + lag)
    def _(i):
        done = lax.rem(jnp.maximum(i - lag, 0) + turn_b, heads)

        if few_b:
            @pl.when(jnp.logical_and(ctx == 1, i == lag))
            def _():
                for x in range(few_b):
                    h = many_b + x
                    early_b(x).wait_recv()
                    grad_local[h, 0] = grad_local[h, 0] + g_early[x] * full[0]
                    for p in range(PARTS_B):
                        bwd_copy(h, p).start()

        @pl.when(i == 3)
        def _():
            @pl.loop(1, ndp)
            def _(d):
                peer = lax.rem(dp + d, ndp)
                dp_copy(peer, peer).wait_recv()

            own = gg_dp[0]
            for n in range(1, ndp):
                own = own + gg_dp[n]
            gg_own[...] = own

        def take(p):
            @pl.when(i >= lag)
            def _():
                take_grad(done, p)

        def intra(j):
            @pl.when(i < heads)
            def _():
                h = i
                at = rows_of(j)
                d = gs[h, at, :]
                dw = (nt(d, vs[h, at, :]) * visible[j]).astype(BF16)
                gq = nn(dw, ks[h, at, :]) + nt(d * mprev[at, :], state_bf[h, j])
                gq_s[h, at, :] = gq.astype(BF16)
                dw_t = (nt(vs[h, at, :], d) * visible_t[j]).astype(BF16)
                att[h, at, :] = nn(dw_t, qs[h, at, :])
                gv_part[h, at, :] = nn(weights_t[h, j], d)

        def finish():
            h = done
            came = g_in[h]
            for j in range(blocks):
                at = rows_of(j)
                grad = came if j == blocks - 1 else grad_local[h, j + 1] + came * full[j + 1]
                grad = grad.astype(BF16)
                ml = mlast[at, :]
                gk_s[h, at, :] = (att[h, at, :] + nt(vs[h, at, :] * ml, grad)).astype(BF16)
                gv_s[h, at, :] = (gv_part[h, at, :] + nn(ks[h, at, :] * ml, grad)).astype(BF16)

        def piece(n):
            if n < blocks:
                intra(n)
            else:
                pl.when(i == down_at)(send_down)
                pl.when(i >= lag)(finish)

        interleave(PARTS_B, take, piece)

        @pl.when(jnp.logical_and(i == up_at, ctx < last))
        def _():
            @pl.when(ctx > 0)
            def _():
                up_copy().wait_recv()
                gg_up_out[...] = gg_own[...] + gg_up_in[...]

            @pl.when(ctx == 0)
            def _():
                gg_up_out[...] = gg_own[...]

            up_copy().start()

    @pl.when(ctx == 0)
    def _():
        @pl.when(ctx < last)
        def _():
            down_copy().wait_recv()
            gg_ref[...] = gg_own[...] + gg_down_in[...]

        @pl.when(ctx == last)
        def _():
            gg_ref[...] = gg_own[...]

    @pl.when(inner)
    def _():
        gg_ref[...] = gg_up_out[...] + gg_down_in[...]

    @pl.when(jnp.logical_and(ctx > 0, ctx == last))
    def _():
        up_copy().wait_recv()
        gg_ref[...] = gg_up_in[...] + gg_own[...]

    pltpu.make_async_remote_copy(
        gg_dp.at[pl.ds(0, ndp - 1)], gg_dp.at[pl.ds(0, ndp - 1)], ds_sem, dr_sem.at[0],
        device_id={"dp": dp}, device_id_type=MESH,
    ).wait_send()

    @pl.when(ctx < last)
    def _():
        tile_copy().wait_send()
        up_copy().wait_send()
        pltpu.make_async_remote_copy(
            s_in, s_in, fs_sem, fr_sem.at[0], device_id=above, device_id_type=MESH
        ).wait_send()

    if few_f:
        @pl.when(ctx == 1)
        def _():
            pltpu.make_async_remote_copy(
                s_early, s_early, es_sem.at[0], ef_sem.at[0], device_id=above, device_id_type=MESH
            ).wait_send()

    if few_b:
        @pl.when(ctx == 2)
        def _():
            pltpu.make_async_remote_copy(
                g_early, g_early, es_sem.at[1], eb_sem.at[0], device_id=below, device_id_type=MESH
            ).wait_send()

    @pl.when(ctx > 0)
    def _():
        down_copy().wait_send()
        pltpu.make_async_remote_copy(
            g_in, g_in, bs_sem, br_sem.at[0], device_id=below, device_id_type=MESH
        ).wait_send()


def writer(heads, *refs):
    sems, gain_sem = refs[10:]
    small = pltpu.make_async_copy(refs[4], refs[9], gain_sem)
    small.start()

    def copy(n, h):
        cols = pl.ds(pl.multiple_of(h * HD, HD), HD)
        return pltpu.make_async_copy(refs[n].at[h], refs[5 + n].at[0, :, cols], sems.at[n, h])

    @pl.loop(0, heads)
    def _(h):
        for n in range(4):
            copy(n, h).start()

    @pl.loop(0, heads)
    def _(h):
        for n in range(4):
            copy(n, h).wait()

    small.wait()


def body(nctx, ndp, full_width, queries, keys_in, values, norm_gain, segment_ids, grad_out):
    toks, local_width = queries.shape[1:]
    heads = local_width // HD
    blocks = toks // BLK
    wide = jax.ShapeDtypeStruct(queries.shape, BF16)
    hbm = pl.BlockSpec(memory_space=pl.ANY)
    vmem = pl.BlockSpec(memory_space=pltpu.VMEM)
    per_head = pltpu.VMEM((heads, toks, HD), BF16)
    states = pltpu.VMEM((heads, blocks, HD, HD), F32)
    hops = pltpu.VMEM((heads, HD, HD), F32)
    ids = segment_ids.shape[1]
    short = nctx == 4 and 2 * ids + 2 > nctx * ids // 2
    few_f, few_b = (EARLY_F, EARLY_B) if short else (0, 0)

    def early(few):
        return pltpu.VMEM((max(few, 1), HD, HD), F32)

    rowish = pltpu.VMEM((toks, HD), F32)
    dma = pltpu.SemaphoreType.DMA
    sums = pltpu.VMEM((2, 8, toks), F32)
    tile = pltpu.VMEM((8, HD), F32)
    gains = pltpu.VMEM((heads, HD), F32)
    outs = pl.pallas_call(
        functools.partial(kernel, nctx, ndp, heads, blocks, full_width, few_f, few_b),
        out_shape=[pltpu.VMEM((heads, toks, HD), BF16)] * 4 + [pltpu.VMEM((heads, HD), F32)],
        in_specs=[hbm] * 6,
        out_specs=[vmem] * 5,
        scratch_shapes=[pltpu.SMEM(segment_ids.shape, jnp.int32), gains]
        + [per_head] * 4
        + [
            pltpu.VMEM((heads, toks, HD), F32),
            pltpu.VMEM((heads, toks, HD), F32),
            pltpu.VMEM((heads, blocks, BLK, BLK), BF16),
            pltpu.VMEM((blocks, BLK, BLK), F32),
            pltpu.VMEM((blocks, BLK, BLK), F32),
            pltpu.VMEM((toks, HD), BF16),
            pltpu.VMEM((toks, HD), BF16),
            states,
            pltpu.VMEM((heads, blocks, HD, HD), BF16),
            hops, early(few_f), states, hops, early(few_b),
            rowish, rowish,
            tile, tile, sums, sums,
            gains, pltpu.VMEM((ndp, heads, HD), F32),
            gains, gains, gains, gains, gains, tile,
            dma((6,)),
            dma, dma((heads * PARTS_F,)), dma, dma((heads * PARTS_B,)),
            dma((2,)), dma((max(few_f, 1),)), dma((max(few_b, 1),)),
            dma, dma, dma, dma,
            dma, dma((ndp,)), dma((2,)), dma((2,)),
        ],
        compiler_params=pltpu.CompilerParams(
            collective_id=0, has_side_effects=True, vmem_limit_bytes=55 << 20
        ),
    )(segment_ids, norm_gain.reshape(heads, HD), queries, keys_in, values, grad_out)
    copies = pl.pallas_call(
        functools.partial(writer, heads),
        out_shape=[wide] * 4 + [jax.ShapeDtypeStruct((heads, HD), F32)],
        in_specs=[hbm] * 5,
        out_specs=[hbm] * 5,
        scratch_shapes=[dma((4, heads)), dma],
        compiler_params=pltpu.CompilerParams(vmem_limit_bytes=1 << 20),
    )(*outs)
    return (*copies[:4], copies[4].reshape(local_width))


def solution(mesh):
    wide = P("dp", "context", "tensor")
    in_specs = (wide, wide, wide, P("tensor"), P("dp", "context"), wide)
    out_specs = (wide, wide, wide, wide, P("tensor"))

    def run(queries, *rest):
        fn = functools.partial(
            body, mesh.shape["context"], mesh.shape["dp"], queries.shape[2]
        )
        return jax.shard_map(
            fn, mesh=mesh, in_specs=in_specs, out_specs=out_specs, check_vma=False
        )(queries, *rest)

    return run
```

```python
import functools

import jax
import jax.numpy as jnp
from jax import lax
from jax.experimental import pallas as pl
from jax.experimental.pallas import tpu as pltpu
from jax.sharding import PartitionSpec as P

HD = 128
BLK = 256
SEGB = 64
PARTS_F = 2
PARTS_B = 1
EARLY_F = 2
EARLY_B = 3
PER = BLK // SEGB
F32 = jnp.float32
BF16 = jnp.bfloat16
MESH = pl.DeviceIdType.MESH


def nn(a, b):
    return lax.dot_general(a, b, (((1,), (0,)), ((), ())), preferred_element_type=F32)


def nt(a, b):
    return lax.dot_general(a, b, (((1,), (1,)), ((), ())), preferred_element_type=F32)


def tn(a, b):
    return lax.dot_general(a, b, (((0,), (0,)), ((), ())), preferred_element_type=F32)


def flag(cond):
    return jnp.where(cond, 1.0, 0.0).astype(F32)


def spread(index, ids):
    out = jnp.full(index.shape, ids[-1], jnp.int32)
    for i in reversed(range(len(ids) - 1)):
        out = jnp.where(index < (i + 1) * SEGB, ids[i], out)
    return out


def kernel(
    nctx, ndp, heads, blocks, width, few_f, few_b,
    seg_hbm, gain_hbm, q_hbm, k_hbm, v_hbm, g_hbm,
    no_s, gq_s, gk_s, gv_s, gg_ref,
    seg_ref, gain_ref, qs, ks, vs, gs,
    att, gv_part, weights_t, visible, visible_t, mprev, mlast,
    local, state_bf, s_in, s_early, grad_local, g_in, g_early,
    sq_acc, in_acc, tile_out, tile_in, sums_out, sums_in,
    gg_part, gg_dp, gg_own, gg_down_out, gg_down_in, gg_up_out, gg_up_in, match_ref,
    in_sem, fs_sem, fr_sem, bs_sem, br_sem, es_sem, ef_sem, eb_sem, ts_sem, tr_sem,
    xs_sem, xr_sem, ds_sem, dr_sem, cs_sem, cr_sem,
):
    ctx = lax.axis_index("context")
    ten = lax.axis_index("tensor")
    dp = lax.axis_index("dp")
    toks = blocks * BLK
    last = nctx - 1
    below = {"context": jnp.maximum(ctx - 1, 0)}
    above = {"context": jnp.minimum(ctx + 1, last)}
    inner = jnp.logical_and(ctx > 0, ctx < last)
    many_f, many_b = heads - few_f, heads - few_b

    barrier = pltpu.get_barrier_semaphore()

    @pl.when(ctx > 0)
    def _():
        pl.semaphore_signal(barrier, inc=1, device_id=below, device_id_type=MESH)

    @pl.when(ctx < last)
    def _():
        pl.semaphore_signal(barrier, inc=1, device_id=above, device_id_type=MESH)

    pl.semaphore_signal(barrier, inc=1, device_id={"tensor": 1 - ten}, device_id_type=MESH)

    @pl.loop(1, ndp)
    def _(d):
        pl.semaphore_signal(
            barrier, inc=1, device_id={"dp": lax.rem(dp + d, ndp)}, device_id_type=MESH
        )

    seg_copy = pltpu.make_async_copy(seg_hbm, seg_ref, in_sem.at[4])
    gain_copy = pltpu.make_async_copy(gain_hbm, gain_ref, in_sem.at[5])
    seg_copy.start()
    gain_copy.start()

    ins = ((k_hbm, ks), (v_hbm, vs), (q_hbm, qs), (g_hbm, gs))

    def load(n, h, sem):
        src, dst = ins[n]
        cols = pl.ds(pl.multiple_of(h * HD, HD), HD)
        pltpu.make_async_copy(src.at[0, :, cols], dst.at[h], in_sem.at[sem]).start()

    for n in range(4):
        @pl.loop(0, heads)
        def _(h):
            load(n, h, n)

    def arrived(n):
        pltpu.make_async_copy(ins[n][1], ins[n][1], in_sem.at[n]).wait()

    seg_copy.wait()
    seg = [[seg_ref[0, j * PER + i] for i in range(PER)] for j in range(blocks)]
    lasts = [seg[j][-1] for j in range(blocks)]
    tile_out[...] = jnp.full((8, HD), lasts[-1], jnp.int32).astype(F32)
    rows_h = lax.broadcasted_iota(jnp.int32, (BLK, HD), 0)
    step = [flag(seg[0][0] == lasts[0])]
    for j in range(1, blocks):
        step.append(flag(lasts[j - 1] == lasts[j]))

    def rows_of(j):
        return pl.ds(j * BLK, BLK)

    for j in range(blocks):
        seg_h = spread(rows_h, seg[j])
        mlast[rows_of(j), :] = flag(seg_h == lasts[j]).astype(BF16)
        before = seg[0][0] if j == 0 else lasts[j - 1]
        mprev[rows_of(j), :] = flag(seg_h == before).astype(BF16)

    def tile_copy():
        return pltpu.make_async_remote_copy(
            tile_out, tile_in, ts_sem, tr_sem, device_id=above, device_id_type=MESH
        )

    def part(p, parts):
        return pl.ds(p * (HD // parts), HD // parts)

    def fwd_copy(h, p, src=None):
        src = local.at[h, blocks - 1] if src is None else src
        return pltpu.make_async_remote_copy(
            src.at[part(p, PARTS_F)], s_in.at[h, part(p, PARTS_F)], fs_sem,
            fr_sem.at[h * PARTS_F + p], device_id=above, device_id_type=MESH,
        )

    def bwd_copy(h, p, src=None):
        src = grad_local.at[h, 0] if src is None else src
        return pltpu.make_async_remote_copy(
            src.at[part(p, PARTS_B)], g_in.at[h, part(p, PARTS_B)], bs_sem,
            br_sem.at[h * PARTS_B + p], device_id=below, device_id_type=MESH,
        )

    def early_f(x):
        return pltpu.make_async_remote_copy(
            local.at[many_f + x, blocks - 1], s_early.at[x], es_sem.at[0],
            ef_sem.at[x], device_id=above, device_id_type=MESH,
        )

    def early_b(x):
        return pltpu.make_async_remote_copy(
            grad_local.at[many_b + x, 0], g_early.at[x], es_sem.at[1],
            eb_sem.at[x], device_id=below, device_id_type=MESH,
        )

    def local_sums(h):
        run = None
        for j in range(blocks):
            km = ks[h, rows_of(j), :] * mlast[rows_of(j), :]
            add = tn(km, vs[h, rows_of(j), :])
            run = add if run is None else run * step[j] + add
            local[h, j] = run

    def scores(h, j):
        at = rows_of(j)
        w = (nt(qs[h, at, :], ks[h, at, :]) * visible[j]).astype(BF16)
        w_t = nt(ks[h, at, :], qs[h, at, :]) * visible_t[j]
        weights_t[h, j] = w_t.astype(BF16)
        att[h, at, :] = nn(w, vs[h, at, :])

    def interleave(parts, take, piece):
        for n in range(blocks + 1):
            for p in range(parts):
                if p * (blocks + 1) // parts == n:
                    take(p)
            piece(n)

    def first_send(h):
        @pl.when(jnp.logical_and(ctx == 0, ctx < last))
        def _():
            for p in range(PARTS_F):
                fwd_copy(h, p).start()

    rows = lax.broadcasted_iota(jnp.int32, (BLK, BLK), 0)
    cols = lax.broadcasted_iota(jnp.int32, (BLK, BLK), 1)
    for j in range(blocks):
        same = spread(rows, seg[j]) == spread(cols, seg[j])
        visible[j] = flag(jnp.logical_and(rows >= cols, same))
        visible_t[j] = flag(jnp.logical_and(cols >= rows, same))
    sq_acc[...] = jnp.zeros_like(sq_acc)
    in_acc[...] = jnp.zeros_like(in_acc)

    @pl.when(ctx == 0)
    def _():
        s_in[...] = jnp.zeros_like(s_in)
        tile_in[...] = jnp.full((8, HD), -1.0, F32)

    @pl.when(ctx == last)
    def _():
        g_in[...] = jnp.zeros_like(g_in)

    arrived(0)
    arrived(1)
    local_sums(0)
    for x in range(few_f):
        local_sums(many_f + x)

    pl.semaphore_wait(
        barrier,
        ndp + jnp.where(ctx > 0, 1, 0) + jnp.where(ctx < last, 1, 0),
    )

    @pl.when(ctx < last)
    def _():
        tile_copy().start()

    first_send(0)

    if few_f:
        @pl.when(ctx == 1)
        def _():
            for x in range(few_f):
                early_f(x).start()

    @pl.loop(1, many_f)
    def _(h):
        local_sums(h)
        first_send(h)

    for x in range(few_f):
        first_send(many_f + x)

    arrived(2)
    turn_f = jnp.where(ctx == last, many_f, 0)
    for j in range(blocks):
        scores(lax.rem(turn_f, heads), j)
    gain_copy.wait()
    arrived(3)

    @pl.when(ctx > 0)
    def _():
        tile_copy().wait_recv()

    first = jnp.full((1, HD), seg[0][0], jnp.int32).astype(F32)
    match = flag(tile_in[0:1, :] == first)
    at0 = rows_of(0)
    mprev[at0, :] = (mprev[at0, :].astype(F32) * match).astype(BF16)
    reach = [match * step[0]]
    for j in range(1, blocks):
        reach.append(reach[-1] * step[j])

    if few_f:
        @pl.when(ctx == 2)
        def _():
            for x in range(few_f):
                h = many_f + x
                early_f(x).wait_recv()
                local[h, blocks - 1] = local[h, blocks - 1] + s_early[x] * reach[-1]
                for p in range(PARTS_F):
                    fwd_copy(h, p).start()

    def take_state(h, p):
        at = part(p, PARTS_F)

        @pl.when(ctx > 0)
        def _():
            fwd_copy(h, p).wait_recv()

        @pl.when(jnp.logical_and(inner, h < many_f))
        def _():
            local[h, blocks - 1, at, :] = (
                local[h, blocks - 1, at, :] + s_in[h, at, :] * reach[-1]
            )
            fwd_copy(h, p).start()

        if few_f:
            @pl.when(jnp.logical_and(inner, h >= many_f))
            def _():
                x = h - many_f

                @pl.when(ctx == 1)
                def _():
                    s_early[x, at, :] = s_in[h, at, :] * reach[-1]
                    fwd_copy(h, p, s_early.at[x]).start()

                @pl.when(ctx == 2)
                def _():
                    s_in[h, at, :] = s_in[h, at, :] + s_early[x, at, :]

    def attend(h):
        gain = gain_ref[pl.ds(h, 1), :]
        came = s_in[h]
        for j in range(blocks):
            at = rows_of(j)
            state = came if j == 0 else local[h, j - 1] + came * reach[j - 1]
            state = state.astype(BF16)
            state_bf[h, j] = state
            a = att[h, at, :] + nn(qs[h, at, :] * mprev[at, :], state)
            att[h, at, :] = a
            sq_acc[at, :] += a * a
            in_acc[at, :] += a * (gs[h, at, :].astype(F32) * gain)

    @pl.loop(0, heads - 1)
    def _(i):
        h = lax.rem(i + turn_f, heads)
        after = lax.rem(h + 1, heads)

        def piece(n):
            if n < blocks:
                scores(after, n)
            else:
                attend(h)

        interleave(PARTS_F, functools.partial(take_state, h), piece)

    final = lax.rem(heads - 1 + turn_f, heads)
    for p in range(PARTS_F):
        take_state(final, p)
    attend(final)

    ones = jnp.ones((16, HD), BF16)
    for n, acc in ((0, sq_acc), (1, in_acc)):
        whole = acc[...]
        high = whole.astype(BF16)
        low = (whole - high.astype(F32)).astype(BF16)
        sums_out[n] = (nt(ones, high) + nt(ones, low))[0:8, :]
    swap = pltpu.make_async_remote_copy(
        sums_out, sums_in, xs_sem, xr_sem, device_id={"tensor": 1 - ten}, device_id_type=MESH
    )
    swap.start()
    swap.wait_recv()
    total_sq = sums_out[0] + sums_in[0]
    total_in = sums_out[1] + sums_in[1]
    radius = jnp.sqrt(total_sq / width + 1e-06)
    inv = 1.0 / radius
    level = lax.broadcasted_iota(jnp.int32, (8, toks), 0)
    for acc, row in ((sq_acc, inv), (in_acc, total_in / (width * radius * radius) * inv)):
        high = row.astype(BF16).astype(F32)
        low = row - high
        middle = low.astype(BF16).astype(F32)
        split = jnp.where(level == 0, high, jnp.where(level == 1, middle, low - middle))
        split = jnp.where(level < 3, split, 0.0)
        split = jnp.concatenate([split, jnp.zeros_like(split)], axis=0).astype(BF16)
        acc[...] = tn(split, ones)

    keep = [match * step[0]] + step[1:]
    full = [None] * (blocks + 1)
    full[blocks] = 1.0
    for j in reversed(range(blocks)):
        full[j] = full[j + 1] * keep[j]

    first_rest = min(many_b, 5)

    @pl.loop(0, heads)
    def _(i):
        h = lax.rem(i + jnp.where(ctx == 2, many_b, 0), heads)
        gain = gain_ref[pl.ds(h, 1), :]
        total = jnp.zeros((1, HD), F32)
        adds = []
        for j in range(blocks):
            at = rows_of(j)
            inv = sq_acc[at, :]
            a = att[h, at, :]
            g = gs[h, at, :].astype(F32)
            normed = a * inv
            no_s[h, at, :] = (normed * gain).astype(BF16)
            total = total + jnp.sum(g * normed, axis=0, keepdims=True)
            d = (g * gain * inv - a * in_acc[at, :]).astype(BF16)
            gs[h, at, :] = d
            adds.append(tn(qs[h, at, :] * mprev[at, :], d))
        gg_part[pl.ds(h, 1), :] = total
        run = None
        for j in reversed(range(blocks)):
            run = adds[j] if run is None else adds[j] + run * keep[j]
            grad_local[h, j] = run

        @pl.when(jnp.logical_and(ctx == last, jnp.logical_and(ctx > 0, h < first_rest)))
        def _():
            for p in range(PARTS_B):
                bwd_copy(h, p).start()

        if few_b:
            @pl.when(jnp.logical_and(ctx == 2, h >= many_b))
            def _():
                early_b(h - many_b).start()

    def dp_copy(to, slot):
        return pltpu.make_async_remote_copy(
            gg_part, gg_dp.at[slot], ds_sem, dr_sem.at[slot],
            device_id={"dp": to}, device_id_type=MESH,
        )

    gg_dp[dp] = gg_part[...]

    @pl.loop(1, ndp)
    def _(d):
        dp_copy(lax.rem(dp + d, ndp), dp).start()

    def down_copy():
        return pltpu.make_async_remote_copy(
            gg_down_out, gg_down_in, cs_sem.at[0], cr_sem.at[0], device_id=below, device_id_type=MESH
        )

    def up_copy():
        return pltpu.make_async_remote_copy(
            gg_up_out, gg_up_in, cs_sem.at[1], cr_sem.at[1], device_id=above, device_id_type=MESH
        )

    def take_grad(h, p):
        at = part(p, PARTS_B)

        @pl.when(ctx < last)
        def _():
            bwd_copy(h, p).wait_recv()

        @pl.when(jnp.logical_and(inner, h < many_b))
        def _():
            grad_local[h, 0, at, :] = grad_local[h, 0, at, :] + g_in[h, at, :] * full[0]
            bwd_copy(h, p).start()

        if few_b:
            @pl.when(jnp.logical_and(inner, h >= many_b))
            def _():
                x = h - many_b

                @pl.when(ctx == 2)
                def _():
                    g_early[x, at, :] = g_in[h, at, :] * full[0]
                    bwd_copy(h, p, g_early.at[x]).start()

                @pl.when(ctx == 1)
                def _():
                    g_in[h, at, :] = g_in[h, at, :] + g_early[x, at, :]

    def send_down():
        @pl.when(inner)
        def _():
            down_copy().wait_recv()
            gg_down_out[...] = gg_own[...] + gg_down_in[...]

        @pl.when(jnp.logical_and(ctx > 0, ctx == last))
        def _():
            gg_down_out[...] = gg_own[...]

        @pl.when(ctx > 0)
        def _():
            down_copy().start()

        @pl.when(jnp.logical_and(ctx > 0, ctx == last))
        def _():
            for h in range(first_rest, heads):
                for p in range(PARTS_B):
                    bwd_copy(h, p).start()

    lag = jnp.where(ctx == 0, heads, jnp.clip(2 * (last - ctx) - 1, 0, heads))
    turn_b = jnp.where(ctx == 0, many_b, 0)
    down_at = lag + jnp.where(ctx == last, min(3, heads - 1), first_rest - 1)
    up_at = jnp.clip(3 * ctx, 3, heads + lag - 1)

    @pl.loop(0, heads + lag)
    def _(i):
        done = lax.rem(jnp.maximum(i - lag, 0) + turn_b, heads)

        if few_b:
            @pl.when(jnp.logical_and(ctx == 1, i == lag))
            def _():
                for x in range(few_b):
                    h = many_b + x
                    early_b(x).wait_recv()
                    grad_local[h, 0] = grad_local[h, 0] + g_early[x] * full[0]
                    for p in range(PARTS_B):
                        bwd_copy(h, p).start()

        @pl.when(i == 3)
        def _():
            @pl.loop(1, ndp)
            def _(d):
                peer = lax.rem(dp + d, ndp)
                dp_copy(peer, peer).wait_recv()

            own = gg_dp[0]
            for n in range(1, ndp):
                own = own + gg_dp[n]
            gg_own[...] = own

        def take(p):
            @pl.when(i >= lag)
            def _():
                take_grad(done, p)

        def intra(j):
            @pl.when(i < heads)
            def _():
                h = i
                at = rows_of(j)
                d = gs[h, at, :]
                dw = (nt(d, vs[h, at, :]) * visible[j]).astype(BF16)
                gq = nn(dw, ks[h, at, :]) + nt(d * mprev[at, :], state_bf[h, j])
                gq_s[h, at, :] = gq.astype(BF16)
                dw_t = (nt(vs[h, at, :], d) * visible_t[j]).astype(BF16)
                att[h, at, :] = nn(dw_t, qs[h, at, :])
                gv_part[h, at, :] = nn(weights_t[h, j], d)

        def finish():
            h = done
            came = g_in[h]
            for j in range(blocks):
                at = rows_of(j)
                grad = came if j == blocks - 1 else grad_local[h, j + 1] + came * full[j + 1]
                grad = grad.astype(BF16)
                ml = mlast[at, :]
                gk_s[h, at, :] = (att[h, at, :] + nt(vs[h, at, :] * ml, grad)).astype(BF16)
                gv_s[h, at, :] = (gv_part[h, at, :] + nn(ks[h, at, :] * ml, grad)).astype(BF16)

        def piece(n):
            if n < blocks:
                intra(n)
            else:
                pl.when(i == down_at)(send_down)
                pl.when(i >= lag)(finish)

        interleave(PARTS_B, take, piece)

        @pl.when(jnp.logical_and(i == up_at, ctx < last))
        def _():
            @pl.when(ctx > 0)
            def _():
                up_copy().wait_recv()
                gg_up_out[...] = gg_own[...] + gg_up_in[...]

            @pl.when(ctx == 0)
            def _():
                gg_up_out[...] = gg_own[...]

            up_copy().start()

    @pl.when(ctx == 0)
    def _():
        @pl.when(ctx < last)
        def _():
            down_copy().wait_recv()
            gg_ref[...] = gg_own[...] + gg_down_in[...]

        @pl.when(ctx == last)
        def _():
            gg_ref[...] = gg_own[...]

    @pl.when(inner)
    def _():
        gg_ref[...] = gg_up_out[...] + gg_down_in[...]

    @pl.when(jnp.logical_and(ctx > 0, ctx == last))
    def _():
        up_copy().wait_recv()
        gg_ref[...] = gg_up_in[...] + gg_own[...]

    swap.wait_send()
    pltpu.make_async_remote_copy(
        gg_dp.at[pl.ds(0, ndp - 1)], gg_dp.at[pl.ds(0, ndp - 1)], ds_sem, dr_sem.at[0],
        device_id={"dp": dp}, device_id_type=MESH,
    ).wait_send()

    @pl.when(ctx < last)
    def _():
        tile_copy().wait_send()
        up_copy().wait_send()
        pltpu.make_async_remote_copy(
            s_in, s_in, fs_sem, fr_sem.at[0], device_id=above, device_id_type=MESH
        ).wait_send()

    if few_f:
        @pl.when(ctx == 1)
        def _():
            pltpu.make_async_remote_copy(
                s_early, s_early, es_sem.at[0], ef_sem.at[0], device_id=above, device_id_type=MESH
            ).wait_send()

    if few_b:
        @pl.when(ctx == 2)
        def _():
            pltpu.make_async_remote_copy(
                g_early, g_early, es_sem.at[1], eb_sem.at[0], device_id=below, device_id_type=MESH
            ).wait_send()

    @pl.when(ctx > 0)
    def _():
        down_copy().wait_send()
        pltpu.make_async_remote_copy(
            g_in, g_in, bs_sem, br_sem.at[0], device_id=below, device_id_type=MESH
        ).wait_send()


def writer(heads, *refs):
    sems, gain_sem = refs[10:]
    small = pltpu.make_async_copy(refs[4], refs[9], gain_sem)
    small.start()

    def copy(n, h):
        cols = pl.ds(pl.multiple_of(h * HD, HD), HD)
        return pltpu.make_async_copy(refs[n].at[h], refs[5 + n].at[0, :, cols], sems.at[n, h])

    @pl.loop(0, heads)
    def _(h):
        for n in range(4):
            copy(n, h).start()

    @pl.loop(0, heads)
    def _(h):
        for n in range(4):
            copy(n, h).wait()

    small.wait()


def body(nctx, ndp, full_width, queries, keys_in, values, norm_gain, segment_ids, grad_out):
    toks, local_width = queries.shape[1:]
    heads = local_width // HD
    blocks = toks // BLK
    wide = jax.ShapeDtypeStruct(queries.shape, BF16)
    hbm = pl.BlockSpec(memory_space=pl.ANY)
    vmem = pl.BlockSpec(memory_space=pltpu.VMEM)
    per_head = pltpu.VMEM((heads, toks, HD), BF16)
    states = pltpu.VMEM((heads, blocks, HD, HD), F32)
    hops = pltpu.VMEM((heads, HD, HD), F32)
    ids = segment_ids.shape[1]
    short = nctx == 4 and 2 * ids + 2 > nctx * ids // 2
    few_f, few_b = (EARLY_F, EARLY_B) if short else (0, 0)

    def early(few):
        return pltpu.VMEM((max(few, 1), HD, HD), F32)

    rowish = pltpu.VMEM((toks, HD), F32)
    dma = pltpu.SemaphoreType.DMA
    sums = pltpu.VMEM((2, 8, toks), F32)
    tile = pltpu.VMEM((8, HD), F32)
    gains = pltpu.VMEM((heads, HD), F32)
    outs = pl.pallas_call(
        functools.partial(kernel, nctx, ndp, heads, blocks, full_width, few_f, few_b),
        out_shape=[pltpu.VMEM((heads, toks, HD), BF16)] * 4 + [pltpu.VMEM((heads, HD), F32)],
        in_specs=[hbm] * 6,
        out_specs=[vmem] * 5,
        scratch_shapes=[pltpu.SMEM(segment_ids.shape, jnp.int32), gains]
        + [per_head] * 4
        + [
            pltpu.VMEM((heads, toks, HD), F32),
            pltpu.VMEM((heads, toks, HD), F32),
            pltpu.VMEM((heads, blocks, BLK, BLK), BF16),
            pltpu.VMEM((blocks, BLK, BLK), F32),
            pltpu.VMEM((blocks, BLK, BLK), F32),
            pltpu.VMEM((toks, HD), BF16),
            pltpu.VMEM((toks, HD), BF16),
            states,
            pltpu.VMEM((heads, blocks, HD, HD), BF16),
            hops, early(few_f), states, hops, early(few_b),
            rowish, rowish,
            tile, tile, sums, sums,
            gains, pltpu.VMEM((ndp, heads, HD), F32),
            gains, gains, gains, gains, gains, tile,
            dma((6,)),
            dma, dma((heads * PARTS_F,)), dma, dma((heads * PARTS_B,)),
            dma((2,)), dma((max(few_f, 1),)), dma((max(few_b, 1),)),
            dma, dma, dma, dma,
            dma, dma((ndp,)), dma((2,)), dma((2,)),
        ],
        compiler_params=pltpu.CompilerParams(
            collective_id=0, has_side_effects=True, vmem_limit_bytes=55 << 20
        ),
    )(segment_ids, norm_gain.reshape(heads, HD), queries, keys_in, values, grad_out)
    copies = pl.pallas_call(
        functools.partial(writer, heads),
        out_shape=[wide] * 4 + [jax.ShapeDtypeStruct((heads, HD), F32)],
        in_specs=[hbm] * 5,
        out_specs=[hbm] * 5,
        scratch_shapes=[dma((4, heads)), dma],
        compiler_params=pltpu.CompilerParams(vmem_limit_bytes=1 << 20),
    )(*outs)
    return (*copies[:4], copies[4].reshape(local_width))


def solution(mesh):
    wide = P("dp", "context", "tensor")
    in_specs = (wide, wide, wide, P("tensor"), P("dp", "context"), wide)
    out_specs = (wide, wide, wide, wide, P("tensor"))

    def run(queries, *rest):
        fn = functools.partial(
            body, mesh.shape["context"], mesh.shape["dp"], queries.shape[2]
        )
        return jax.shard_map(
            fn, mesh=mesh, in_specs=in_specs, out_specs=out_specs, check_vma=False
        )(queries, *rest)

    return run
```

```python
import functools

import jax
import jax.numpy as jnp
from jax import lax
from jax.experimental import pallas as pl
from jax.experimental.pallas import tpu as pltpu
from jax.sharding import PartitionSpec as P

HD = 128
BLK = 256
SEGB = 64
PARTS_F = 2
PARTS_B = 1
EARLY_F = 2
EARLY_B = 3
PER = BLK // SEGB
F32 = jnp.float32
BF16 = jnp.bfloat16
MESH = pl.DeviceIdType.MESH


def nn(a, b):
    return lax.dot_general(a, b, (((1,), (0,)), ((), ())), preferred_element_type=F32)


def nt(a, b):
    return lax.dot_general(a, b, (((1,), (1,)), ((), ())), preferred_element_type=F32)


def tn(a, b):
    return lax.dot_general(a, b, (((0,), (0,)), ((), ())), preferred_element_type=F32)


def flag(cond):
    return jnp.where(cond, 1.0, 0.0).astype(F32)


def spread(index, ids):
    out = jnp.full(index.shape, ids[-1], jnp.int32)
    for i in reversed(range(len(ids) - 1)):
        out = jnp.where(index < (i + 1) * SEGB, ids[i], out)
    return out


def kernel(
    nctx, ndp, heads, blocks, width, few_f, few_b,
    seg_hbm, gain_hbm, q_hbm, k_hbm, v_hbm, g_hbm,
    no_s, gq_s, gk_s, gv_s, gg_ref,
    seg_ref, gain_ref, qs, ks, vs, gs,
    att, gv_part, weights_t, visible, visible_t, mprev, mlast,
    local, state_bf, s_in, s_early, grad_local, g_in, g_early,
    sq_acc, in_acc, tile_out, tile_in, sums_out, sums_in,
    gg_part, gg_dp, gg_own, gg_down_out, gg_down_in, gg_up_out, gg_up_in, match_ref,
    in_sem, fs_sem, fr_sem, bs_sem, br_sem, es_sem, ef_sem, eb_sem, ts_sem, tr_sem,
    xs_sem, xr_sem, ds_sem, dr_sem, cs_sem, cr_sem,
):
    ctx = lax.axis_index("context")
    ten = lax.axis_index("tensor")
    dp = lax.axis_index("dp")
    toks = blocks * BLK
    last = nctx - 1
    below = {"context": jnp.maximum(ctx - 1, 0)}
    above = {"context": jnp.minimum(ctx + 1, last)}
    inner = jnp.logical_and(ctx > 0, ctx < last)
    many_f, many_b = heads - few_f, heads - few_b

    barrier = pltpu.get_barrier_semaphore()

    @pl.when(ctx > 0)
    def _():
        pl.semaphore_signal(barrier, inc=1, device_id=below, device_id_type=MESH)

    @pl.when(ctx < last)
    def _():
        pl.semaphore_signal(barrier, inc=1, device_id=above, device_id_type=MESH)

    pl.semaphore_signal(barrier, inc=1, device_id={"tensor": 1 - ten}, device_id_type=MESH)

    @pl.loop(1, ndp)
    def _(d):
        pl.semaphore_signal(
            barrier, inc=1, device_id={"dp": lax.rem(dp + d, ndp)}, device_id_type=MESH
        )

    seg_copy = pltpu.make_async_copy(seg_hbm, seg_ref, in_sem.at[4])
    gain_copy = pltpu.make_async_copy(gain_hbm, gain_ref, in_sem.at[5])
    seg_copy.start()
    gain_copy.start()

    ins = ((k_hbm, ks), (v_hbm, vs), (q_hbm, qs), (g_hbm, gs))

    def load(n, h, sem):
        src, dst = ins[n]
        cols = pl.ds(pl.multiple_of(h * HD, HD), HD)
        pltpu.make_async_copy(src.at[0, :, cols], dst.at[h], in_sem.at[sem]).start()

    for n in range(4):
        @pl.loop(0, heads)
        def _(h):
            load(n, h, n)

    def arrived(n):
        pltpu.make_async_copy(ins[n][1], ins[n][1], in_sem.at[n]).wait()

    seg_copy.wait()
    seg = [[seg_ref[0, j * PER + i] for i in range(PER)] for j in range(blocks)]
    lasts = [seg[j][-1] for j in range(blocks)]
    tile_out[...] = jnp.full((8, HD), lasts[-1], jnp.int32).astype(F32)
    rows_h = lax.broadcasted_iota(jnp.int32, (BLK, HD), 0)
    step = [flag(seg[0][0] == lasts[0])]
    for j in range(1, blocks):
        step.append(flag(lasts[j - 1] == lasts[j]))

    def rows_of(j):
        return pl.ds(j * BLK, BLK)

    for j in range(blocks):
        seg_h = spread(rows_h, seg[j])
        mlast[rows_of(j), :] = flag(seg_h == lasts[j]).astype(BF16)
        before = seg[0][0] if j == 0 else lasts[j - 1]
        mprev[rows_of(j), :] = flag(seg_h == before).astype(BF16)

    def tile_copy():
        return pltpu.make_async_remote_copy(
            tile_out, tile_in, ts_sem, tr_sem, device_id=above, device_id_type=MESH
        )

    def part(p, parts):
        return pl.ds(p * (HD // parts), HD // parts)

    def fwd_copy(h, p, src=None):
        src = local.at[h, blocks - 1] if src is None else src
        return pltpu.make_async_remote_copy(
            src.at[part(p, PARTS_F)], s_in.at[h, part(p, PARTS_F)], fs_sem,
            fr_sem.at[h * PARTS_F + p], device_id=above, device_id_type=MESH,
        )

    def bwd_copy(h, p, src=None):
        src = grad_local.at[h, 0] if src is None else src
        return pltpu.make_async_remote_copy(
            src.at[part(p, PARTS_B)], g_in.at[h, part(p, PARTS_B)], bs_sem,
            br_sem.at[h * PARTS_B + p], device_id=below, device_id_type=MESH,
        )

    def early_f(x):
        return pltpu.make_async_remote_copy(
            local.at[many_f + x, blocks - 1], s_early.at[x], es_sem.at[0],
            ef_sem.at[x], device_id=above, device_id_type=MESH,
        )

    def early_b(x):
        return pltpu.make_async_remote_copy(
            grad_local.at[many_b + x, 0], g_early.at[x], es_sem.at[1],
            eb_sem.at[x], device_id=below, device_id_type=MESH,
        )

    def local_sums(h):
        run = None
        for j in range(blocks):
            km = ks[h, rows_of(j), :] * mlast[rows_of(j), :]
            add = tn(km, vs[h, rows_of(j), :])
            run = add if run is None else run * step[j] + add
            local[h, j] = run

    def scores(h, j):
        at = rows_of(j)
        w = (nt(qs[h, at, :], ks[h, at, :]) * visible[j]).astype(BF16)
        w_t = nt(ks[h, at, :], qs[h, at, :]) * visible_t[j]
        weights_t[h, j] = w_t.astype(BF16)
        att[h, at, :] = nn(w, vs[h, at, :])

    def interleave(parts, take, piece):
        for n in range(blocks + 1):
            for p in range(parts):
                if p * (blocks + 1) // parts == n:
                    take(p)
            piece(n)

    def first_send(h):
        @pl.when(jnp.logical_and(ctx == 0, ctx < last))
        def _():
            for p in range(PARTS_F):
                fwd_copy(h, p).start()

    rows = lax.broadcasted_iota(jnp.int32, (BLK, BLK), 0)
    cols = lax.broadcasted_iota(jnp.int32, (BLK, BLK), 1)
    for j in range(blocks):
        same = spread(rows, seg[j]) == spread(cols, seg[j])
        visible[j] = flag(jnp.logical_and(rows >= cols, same))
        visible_t[j] = flag(jnp.logical_and(cols >= rows, same))
    sq_acc[...] = jnp.zeros_like(sq_acc)
    in_acc[...] = jnp.zeros_like(in_acc)

    @pl.when(ctx == 0)
    def _():
        s_in[...] = jnp.zeros_like(s_in)
        tile_in[...] = jnp.full((8, HD), -1.0, F32)

    @pl.when(ctx == last)
    def _():
        g_in[...] = jnp.zeros_like(g_in)

    arrived(0)
    arrived(1)
    local_sums(0)
    for x in range(few_f):
        local_sums(many_f + x)

    pl.semaphore_wait(
        barrier,
        ndp + jnp.where(ctx > 0, 1, 0) + jnp.where(ctx < last, 1, 0),
    )

    @pl.when(ctx < last)
    def _():
        tile_copy().start()

    first_send(0)

    if few_f:
        @pl.when(ctx == 1)
        def _():
            for x in range(few_f):
                early_f(x).start()

    @pl.loop(1, many_f)
    def _(h):
        local_sums(h)
        first_send(h)

    for x in range(few_f):
        first_send(many_f + x)

    arrived(2)
    turn_f = jnp.where(ctx == last, many_f, 0)
    for j in range(blocks):
        scores(lax.rem(turn_f, heads), j)
    gain_copy.wait()
    arrived(3)

    @pl.when(ctx > 0)
    def _():
        tile_copy().wait_recv()

    first = jnp.full((1, HD), seg[0][0], jnp.int32).astype(F32)
    match = flag(tile_in[0:1, :] == first)
    at0 = rows_of(0)
    mprev[at0, :] = (mprev[at0, :].astype(F32) * match).astype(BF16)
    reach = [match * step[0]]
    for j in range(1, blocks):
        reach.append(reach[-1] * step[j])

    if few_f:
        @pl.when(ctx == 2)
        def _():
            for x in range(few_f):
                h = many_f + x
                early_f(x).wait_recv()
                local[h, blocks - 1] = local[h, blocks - 1] + s_early[x] * reach[-1]
                for p in range(PARTS_F):
                    fwd_copy(h, p).start()

    def take_state(h, p):
        at = part(p, PARTS_F)

        @pl.when(ctx > 0)
        def _():
            fwd_copy(h, p).wait_recv()

        @pl.when(jnp.logical_and(inner, h < many_f))
        def _():
            local[h, blocks - 1, at, :] = (
                local[h, blocks - 1, at, :] + s_in[h, at, :] * reach[-1]
            )
            fwd_copy(h, p).start()

        if few_f:
            @pl.when(jnp.logical_and(inner, h >= many_f))
            def _():
                x = h - many_f

                @pl.when(ctx == 1)
                def _():
                    s_early[x, at, :] = s_in[h, at, :] * reach[-1]
                    fwd_copy(h, p, s_early.at[x]).start()

                @pl.when(ctx == 2)
                def _():
                    s_in[h, at, :] = s_in[h, at, :] + s_early[x, at, :]

    def attend(h):
        gain = gain_ref[pl.ds(h, 1), :]
        came = s_in[h]
        for j in range(blocks):
            at = rows_of(j)
            state = came if j == 0 else local[h, j - 1] + came * reach[j - 1]
            state = state.astype(BF16)
            state_bf[h, j] = state
            a = att[h, at, :] + nn(qs[h, at, :] * mprev[at, :], state)
            att[h, at, :] = a
            sq_acc[at, :] += a * a
            in_acc[at, :] += a * (gs[h, at, :].astype(F32) * gain)

    @pl.loop(0, heads - 1)
    def _(i):
        h = lax.rem(i + turn_f, heads)
        after = lax.rem(h + 1, heads)

        def piece(n):
            if n < blocks:
                scores(after, n)
            else:
                attend(h)

        interleave(PARTS_F, functools.partial(take_state, h), piece)

    final = lax.rem(heads - 1 + turn_f, heads)
    for p in range(PARTS_F):
        take_state(final, p)
    attend(final)

    ones = jnp.ones((16, HD), BF16)
    for n, acc in ((0, sq_acc), (1, in_acc)):
        whole = acc[...]
        high = whole.astype(BF16)
        low = (whole - high.astype(F32)).astype(BF16)
        sums_out[n] = (nt(ones, high) + nt(ones, low))[0:8, :]
    swap = pltpu.make_async_remote_copy(
        sums_out, sums_in, xs_sem, xr_sem, device_id={"tensor": 1 - ten}, device_id_type=MESH
    )
    swap.start()
    swap.wait_recv()
    total_sq = sums_out[0] + sums_in[0]
    total_in = sums_out[1] + sums_in[1]
    radius = jnp.sqrt(total_sq / width + 1e-06)
    inv = 1.0 / radius
    level = lax.broadcasted_iota(jnp.int32, (8, toks), 0)
    for acc, row in ((sq_acc, inv), (in_acc, total_in / (width * radius * radius) * inv)):
        high = row.astype(BF16).astype(F32)
        low = row - high
        middle = low.astype(BF16).astype(F32)
        split = jnp.where(level == 0, high, jnp.where(level == 1, middle, low - middle))
        split = jnp.where(level < 3, split, 0.0)
        split = jnp.concatenate([split, jnp.zeros_like(split)], axis=0).astype(BF16)
        acc[...] = tn(split, ones)

    keep = [match * step[0]] + step[1:]
    full = [None] * (blocks + 1)
    full[blocks] = 1.0
    for j in reversed(range(blocks)):
        full[j] = full[j + 1] * keep[j]

    first_rest = min(many_b, 5)

    @pl.loop(0, heads)
    def _(i):
        h = lax.rem(i + jnp.where(ctx == 2, many_b, 0), heads)
        gain = gain_ref[pl.ds(h, 1), :]
        total = jnp.zeros((1, HD), F32)
        adds = []
        for j in range(blocks):
            at = rows_of(j)
            inv = sq_acc[at, :]
            a = att[h, at, :]
            g = gs[h, at, :].astype(F32)
            normed = a * inv
            no_s[h, at, :] = (normed * gain).astype(BF16)
            total = total + jnp.sum(g * normed, axis=0, keepdims=True)
            d = (g * gain * inv - a * in_acc[at, :]).astype(BF16)
            gs[h, at, :] = d
            adds.append(tn(qs[h, at, :] * mprev[at, :], d))
        gg_part[pl.ds(h, 1), :] = total
        run = None
        for j in reversed(range(blocks)):
            run = adds[j] if run is None else adds[j] + run * keep[j]
            grad_local[h, j] = run

        @pl.when(jnp.logical_and(ctx == last, jnp.logical_and(ctx > 0, h < first_rest)))
        def _():
            for p in range(PARTS_B):
                bwd_copy(h, p).start()

        if few_b:
            @pl.when(jnp.logical_and(ctx == 2, h >= many_b))
            def _():
                early_b(h - many_b).start()

    def dp_copy(to, slot):
        return pltpu.make_async_remote_copy(
            gg_part, gg_dp.at[slot], ds_sem, dr_sem.at[slot],
            device_id={"dp": to}, device_id_type=MESH,
        )

    gg_dp[dp] = gg_part[...]

    @pl.loop(1, ndp)
    def _(d):
        dp_copy(lax.rem(dp + d, ndp), dp).start()

    def down_copy():
        return pltpu.make_async_remote_copy(
            gg_down_out, gg_down_in, cs_sem.at[0], cr_sem.at[0], device_id=below, device_id_type=MESH
        )

    def up_copy():
        return pltpu.make_async_remote_copy(
            gg_up_out, gg_up_in, cs_sem.at[1], cr_sem.at[1], device_id=above, device_id_type=MESH
        )

    def take_grad(h, p):
        at = part(p, PARTS_B)

        @pl.when(ctx < last)
        def _():
            bwd_copy(h, p).wait_recv()

        @pl.when(jnp.logical_and(inner, h < many_b))
        def _():
            grad_local[h, 0, at, :] = grad_local[h, 0, at, :] + g_in[h, at, :] * full[0]
            bwd_copy(h, p).start()

        if few_b:
            @pl.when(jnp.logical_and(inner, h >= many_b))
            def _():
                x = h - many_b

                @pl.when(ctx == 2)
                def _():
                    g_early[x, at, :] = g_in[h, at, :] * full[0]
                    bwd_copy(h, p, g_early.at[x]).start()

                @pl.when(ctx == 1)
                def _():
                    g_in[h, at, :] = g_in[h, at, :] + g_early[x, at, :]

    def send_down():
        @pl.when(inner)
        def _():
            down_copy().wait_recv()
            gg_down_out[...] = gg_own[...] + gg_down_in[...]

        @pl.when(jnp.logical_and(ctx > 0, ctx == last))
        def _():
            gg_down_out[...] = gg_own[...]

        @pl.when(ctx > 0)
        def _():
            down_copy().start()

        @pl.when(jnp.logical_and(ctx > 0, ctx == last))
        def _():
            for h in range(first_rest, heads):
                for p in range(PARTS_B):
                    bwd_copy(h, p).start()

    lag = jnp.where(ctx == 0, heads, jnp.clip(2 * (last - ctx) - 1, 0, heads))
    turn_b = jnp.where(ctx == 0, many_b, 0)
    own_at = jnp.where(ctx == last, min(2, heads - 1), min(3, heads - 1))
    down_at = jnp.where(ctx == last, -1, lag + first_rest - 1)
    up_at = jnp.clip(3 * ctx, 3, heads + lag - 1)

    @pl.loop(0, heads + lag)
    def _(i):
        done = lax.rem(jnp.maximum(i - lag, 0) + turn_b, heads)

        if few_b:
            @pl.when(jnp.logical_and(ctx == 1, i == lag))
            def _():
                for x in range(few_b):
                    h = many_b + x
                    early_b(x).wait_recv()
                    grad_local[h, 0] = grad_local[h, 0] + g_early[x] * full[0]
                    for p in range(PARTS_B):
                        bwd_copy(h, p).start()

        @pl.when(i == own_at)
        def _():
            @pl.loop(1, ndp)
            def _(d):
                peer = lax.rem(dp + d, ndp)
                dp_copy(peer, peer).wait_recv()

            own = gg_dp[0]
            for n in range(1, ndp):
                own = own + gg_dp[n]
            gg_own[...] = own

        pl.when(jnp.logical_and(i == own_at, ctx == last))(send_down)

        def take(p):
            @pl.when(i >= lag)
            def _():
                take_grad(done, p)

        def intra(j):
            @pl.when(i < heads)
            def _():
                h = i
                at = rows_of(j)
                d = gs[h, at, :]
                dw = (nt(d, vs[h, at, :]) * visible[j]).astype(BF16)
                gq = nn(dw, ks[h, at, :]) + nt(d * mprev[at, :], state_bf[h, j])
                gq_s[h, at, :] = gq.astype(BF16)
                dw_t = (nt(vs[h, at, :], d) * visible_t[j]).astype(BF16)
                att[h, at, :] = nn(dw_t, qs[h, at, :])
                gv_part[h, at, :] = nn(weights_t[h, j], d)

        def finish():
            h = done
            came = g_in[h]
            for j in range(blocks):
                at = rows_of(j)
                grad = came if j == blocks - 1 else grad_local[h, j + 1] + came * full[j + 1]
                grad = grad.astype(BF16)
                ml = mlast[at, :]
                gk_s[h, at, :] = (att[h, at, :] + nt(vs[h, at, :] * ml, grad)).astype(BF16)
                gv_s[h, at, :] = (gv_part[h, at, :] + nn(ks[h, at, :] * ml, grad)).astype(BF16)

        def piece(n):
            if n < blocks:
                intra(n)
            else:
                pl.when(i == down_at)(send_down)
                pl.when(i >= lag)(finish)

        interleave(PARTS_B, take, piece)

        @pl.when(jnp.logical_and(i == up_at, ctx < last))
        def _():
            @pl.when(ctx > 0)
            def _():
                up_copy().wait_recv()
                gg_up_out[...] = gg_own[...] + gg_up_in[...]

            @pl.when(ctx == 0)
            def _():
                gg_up_out[...] = gg_own[...]

            up_copy().start()

    @pl.when(ctx == 0)
    def _():
        @pl.when(ctx < last)
        def _():
            down_copy().wait_recv()
            gg_ref[...] = gg_own[...] + gg_down_in[...]

        @pl.when(ctx == last)
        def _():
            gg_ref[...] = gg_own[...]

    @pl.when(inner)
    def _():
        gg_ref[...] = gg_up_out[...] + gg_down_in[...]

    @pl.when(jnp.logical_and(ctx > 0, ctx == last))
    def _():
        up_copy().wait_recv()
        gg_ref[...] = gg_up_in[...] + gg_own[...]

    swap.wait_send()
    pltpu.make_async_remote_copy(
        gg_dp.at[pl.ds(0, ndp - 1)], gg_dp.at[pl.ds(0, ndp - 1)], ds_sem, dr_sem.at[0],
        device_id={"dp": dp}, device_id_type=MESH,
    ).wait_send()

    @pl.when(ctx < last)
    def _():
        tile_copy().wait_send()
        up_copy().wait_send()
        pltpu.make_async_remote_copy(
            s_in, s_in, fs_sem, fr_sem.at[0], device_id=above, device_id_type=MESH
        ).wait_send()

    if few_f:
        @pl.when(ctx == 1)
        def _():
            pltpu.make_async_remote_copy(
                s_early, s_early, es_sem.at[0], ef_sem.at[0], device_id=above, device_id_type=MESH
            ).wait_send()

    if few_b:
        @pl.when(ctx == 2)
        def _():
            pltpu.make_async_remote_copy(
                g_early, g_early, es_sem.at[1], eb_sem.at[0], device_id=below, device_id_type=MESH
            ).wait_send()

    @pl.when(ctx > 0)
    def _():
        down_copy().wait_send()
        pltpu.make_async_remote_copy(
            g_in, g_in, bs_sem, br_sem.at[0], device_id=below, device_id_type=MESH
        ).wait_send()


def writer(heads, *refs):
    sems, gain_sem = refs[10:]
    small = pltpu.make_async_copy(refs[4], refs[9], gain_sem)
    small.start()

    def copy(n, h):
        cols = pl.ds(pl.multiple_of(h * HD, HD), HD)
        return pltpu.make_async_copy(refs[n].at[h], refs[5 + n].at[0, :, cols], sems.at[n])

    @pl.loop(0, heads)
    def _(h):
        for n in range(4):
            copy(n, h).start()

    for n in range(4):
        pltpu.make_async_copy(refs[n], refs[n], sems.at[n]).wait()

    small.wait()


def body(nctx, ndp, full_width, queries, keys_in, values, norm_gain, segment_ids, grad_out):
    toks, local_width = queries.shape[1:]
    heads = local_width // HD
    blocks = toks // BLK
    wide = jax.ShapeDtypeStruct(queries.shape, BF16)
    hbm = pl.BlockSpec(memory_space=pl.ANY)
    vmem = pl.BlockSpec(memory_space=pltpu.VMEM)
    per_head = pltpu.VMEM((heads, toks, HD), BF16)
    states = pltpu.VMEM((heads, blocks, HD, HD), F32)
    hops = pltpu.VMEM((heads, HD, HD), F32)
    ids = segment_ids.shape[1]
    short = nctx == 4 and 2 * ids + 2 > nctx * ids // 2
    few_f, few_b = (EARLY_F, EARLY_B) if short else (0, 0)

    def early(few):
        return pltpu.VMEM((max(few, 1), HD, HD), F32)

    rowish = pltpu.VMEM((toks, HD), F32)
    dma = pltpu.SemaphoreType.DMA
    sums = pltpu.VMEM((2, 8, toks), F32)
    tile = pltpu.VMEM((8, HD), F32)
    gains = pltpu.VMEM((heads, HD), F32)
    outs = pl.pallas_call(
        functools.partial(kernel, nctx, ndp, heads, blocks, full_width, few_f, few_b),
        out_shape=[pltpu.VMEM((heads, toks, HD), BF16)] * 4 + [pltpu.VMEM((heads, HD), F32)],
        in_specs=[hbm] * 6,
        out_specs=[vmem] * 5,
        scratch_shapes=[pltpu.SMEM(segment_ids.shape, jnp.int32), gains]
        + [per_head] * 4
        + [
            pltpu.VMEM((heads, toks, HD), F32),
            pltpu.VMEM((heads, toks, HD), F32),
            pltpu.VMEM((heads, blocks, BLK, BLK), BF16),
            pltpu.VMEM((blocks, BLK, BLK), F32),
            pltpu.VMEM((blocks, BLK, BLK), F32),
            pltpu.VMEM((toks, HD), BF16),
            pltpu.VMEM((toks, HD), BF16),
            states,
            pltpu.VMEM((heads, blocks, HD, HD), BF16),
            hops, early(few_f), states, hops, early(few_b),
            rowish, rowish,
            tile, tile, sums, sums,
            gains, pltpu.VMEM((ndp, heads, HD), F32),
            gains, gains, gains, gains, gains, tile,
            dma((6,)),
            dma, dma((heads * PARTS_F,)), dma, dma((heads * PARTS_B,)),
            dma((2,)), dma((max(few_f, 1),)), dma((max(few_b, 1),)),
            dma, dma, dma, dma,
            dma, dma((ndp,)), dma((2,)), dma((2,)),
        ],
        compiler_params=pltpu.CompilerParams(
            collective_id=0, has_side_effects=True, vmem_limit_bytes=55 << 20
        ),
    )(segment_ids, norm_gain.reshape(heads, HD), queries, keys_in, values, grad_out)
    copies = pl.pallas_call(
        functools.partial(writer, heads),
        out_shape=[wide] * 4 + [jax.ShapeDtypeStruct((heads, HD), F32)],
        in_specs=[hbm] * 5,
        out_specs=[hbm] * 5,
        scratch_shapes=[dma((4,)), dma],
        compiler_params=pltpu.CompilerParams(vmem_limit_bytes=1 << 20),
    )(*outs)
    return (*copies[:4], copies[4].reshape(local_width))


def solution(mesh):
    wide = P("dp", "context", "tensor")
    in_specs = (wide, wide, wide, P("tensor"), P("dp", "context"), wide)
    out_specs = (wide, wide, wide, wide, P("tensor"))

    def run(queries, *rest):
        fn = functools.partial(
            body, mesh.shape["context"], mesh.shape["dp"], queries.shape[2]
        )
        return jax.shard_map(
            fn, mesh=mesh, in_specs=in_specs, out_specs=out_specs, check_vma=False
        )(queries, *rest)

    return run
```

```python
import functools

import jax
import jax.numpy as jnp
from jax import lax
from jax.experimental import pallas as pl
from jax.experimental.pallas import tpu as pltpu
from jax.sharding import PartitionSpec as P

HD = 128
BLK = 256
SEGB = 64
PARTS_F = 2
PARTS_B = 1
EARLY_F = 2
EARLY_B = 3
PER = BLK // SEGB
F32 = jnp.float32
BF16 = jnp.bfloat16
MESH = pl.DeviceIdType.MESH


def nn(a, b):
    return lax.dot_general(a, b, (((1,), (0,)), ((), ())), preferred_element_type=F32)


def nt(a, b):
    return lax.dot_general(a, b, (((1,), (1,)), ((), ())), preferred_element_type=F32)


def tn(a, b):
    return lax.dot_general(a, b, (((0,), (0,)), ((), ())), preferred_element_type=F32)


def flag(cond):
    return jnp.where(cond, 1.0, 0.0).astype(F32)


def spread(index, ids):
    out = jnp.full(index.shape, ids[-1], jnp.int32)
    for i in reversed(range(len(ids) - 1)):
        out = jnp.where(index < (i + 1) * SEGB, ids[i], out)
    return out


def kernel(
    nctx, ndp, heads, blocks, width, few_f, few_b,
    seg_hbm, gain_hbm, q_hbm, k_hbm, v_hbm, g_hbm,
    no_s, gq_s, gk_s, gv_s, gg_ref,
    seg_ref, gain_ref, qs, ks, vs, gs,
    att, gv_part, weights_t, visible, visible_t, mprev, mlast,
    local, state_bf, s_in, s_early, grad_local, g_in, g_early,
    sq_acc, in_acc, tile_out, tile_in, sums_out, sums_in,
    gg_part, gg_dp, gg_own, gg_down_out, gg_down_in, gg_up_out, gg_up_in, match_ref,
    in_sem, fs_sem, fr_sem, bs_sem, br_sem, es_sem, ef_sem, eb_sem, ts_sem, tr_sem,
    xs_sem, xr_sem, ds_sem, dr_sem, cs_sem, cr_sem,
):
    ctx = lax.axis_index("context")
    ten = lax.axis_index("tensor")
    dp = lax.axis_index("dp")
    toks = blocks * BLK
    last = nctx - 1
    below = {"context": jnp.maximum(ctx - 1, 0)}
    above = {"context": jnp.minimum(ctx + 1, last)}
    inner = jnp.logical_and(ctx > 0, ctx < last)
    many_f, many_b = heads - few_f, heads - few_b

    barrier = pltpu.get_barrier_semaphore()

    @pl.when(ctx > 0)
    def _():
        pl.semaphore_signal(barrier, inc=1, device_id=below, device_id_type=MESH)

    @pl.when(ctx < last)
    def _():
        pl.semaphore_signal(barrier, inc=1, device_id=above, device_id_type=MESH)

    pl.semaphore_signal(barrier, inc=1, device_id={"tensor": 1 - ten}, device_id_type=MESH)

    @pl.loop(1, ndp)
    def _(d):
        pl.semaphore_signal(
            barrier, inc=1, device_id={"dp": lax.rem(dp + d, ndp)}, device_id_type=MESH
        )

    seg_copy = pltpu.make_async_copy(seg_hbm, seg_ref, in_sem.at[4])
    gain_copy = pltpu.make_async_copy(gain_hbm, gain_ref, in_sem.at[5])
    seg_copy.start()
    gain_copy.start()

    ins = ((k_hbm, ks), (v_hbm, vs), (q_hbm, qs), (g_hbm, gs))

    def load(n, h, sem):
        src, dst = ins[n]
        cols = pl.ds(pl.multiple_of(h * HD, HD), HD)
        pltpu.make_async_copy(src.at[0, :, cols], dst.at[h], in_sem.at[sem]).start()

    for n in range(4):
        @pl.loop(0, heads)
        def _(h):
            load(n, h, n)

    def arrived(n):
        pltpu.make_async_copy(ins[n][1], ins[n][1], in_sem.at[n]).wait()

    seg_copy.wait()
    seg = [[seg_ref[0, j * PER + i] for i in range(PER)] for j in range(blocks)]
    lasts = [seg[j][-1] for j in range(blocks)]
    tile_out[...] = jnp.full((8, HD), lasts[-1], jnp.int32).astype(F32)
    rows_h = lax.broadcasted_iota(jnp.int32, (BLK, HD), 0)
    step = [flag(seg[0][0] == lasts[0])]
    for j in range(1, blocks):
        step.append(flag(lasts[j - 1] == lasts[j]))

    def rows_of(j):
        return pl.ds(j * BLK, BLK)

    for j in range(blocks):
        seg_h = spread(rows_h, seg[j])
        mlast[rows_of(j), :] = flag(seg_h == lasts[j]).astype(BF16)
        before = seg[0][0] if j == 0 else lasts[j - 1]
        mprev[rows_of(j), :] = flag(seg_h == before).astype(BF16)

    def tile_copy():
        return pltpu.make_async_remote_copy(
            tile_out, tile_in, ts_sem, tr_sem, device_id=above, device_id_type=MESH
        )

    def part(p, parts):
        return pl.ds(p * (HD // parts), HD // parts)

    def fwd_copy(h, p, src=None):
        src = local.at[h, blocks - 1] if src is None else src
        return pltpu.make_async_remote_copy(
            src.at[part(p, PARTS_F)], s_in.at[h, part(p, PARTS_F)], fs_sem,
            fr_sem.at[h * PARTS_F + p], device_id=above, device_id_type=MESH,
        )

    def bwd_copy(h, p, src=None):
        src = grad_local.at[h, 0] if src is None else src
        return pltpu.make_async_remote_copy(
            src.at[part(p, PARTS_B)], g_in.at[h, part(p, PARTS_B)], bs_sem,
            br_sem.at[h * PARTS_B + p], device_id=below, device_id_type=MESH,
        )

    def early_f(x):
        return pltpu.make_async_remote_copy(
            local.at[many_f + x, blocks - 1], s_early.at[x], es_sem.at[0],
            ef_sem.at[x], device_id=above, device_id_type=MESH,
        )

    def early_b(x):
        return pltpu.make_async_remote_copy(
            grad_local.at[many_b + x, 0], g_early.at[x], es_sem.at[1],
            eb_sem.at[x], device_id=below, device_id_type=MESH,
        )

    def local_sums(h):
        run = None
        for j in range(blocks):
            km = ks[h, rows_of(j), :] * mlast[rows_of(j), :]
            add = tn(km, vs[h, rows_of(j), :])
            run = add if run is None else run * step[j] + add
            local[h, j] = run

    def scores(h, j):
        at = rows_of(j)
        w = (nt(qs[h, at, :], ks[h, at, :]) * visible[j]).astype(BF16)
        w_t = nt(ks[h, at, :], qs[h, at, :]) * visible_t[j]
        weights_t[h, j] = w_t.astype(BF16)
        att[h, at, :] = nn(w, vs[h, at, :])

    def interleave(parts, take, piece):
        for n in range(blocks + 1):
            for p in range(parts):
                if p * (blocks + 1) // parts == n:
                    take(p)
            piece(n)

    def first_send(h):
        @pl.when(jnp.logical_and(ctx == 0, ctx < last))
        def _():
            for p in range(PARTS_F):
                fwd_copy(h, p).start()

    rows = lax.broadcasted_iota(jnp.int32, (BLK, BLK), 0)
    cols = lax.broadcasted_iota(jnp.int32, (BLK, BLK), 1)
    for j in range(blocks):
        same = spread(rows, seg[j]) == spread(cols, seg[j])
        visible[j] = flag(jnp.logical_and(rows >= cols, same))
        visible_t[j] = flag(jnp.logical_and(cols >= rows, same))
    sq_acc[...] = jnp.zeros_like(sq_acc)
    in_acc[...] = jnp.zeros_like(in_acc)

    @pl.when(ctx == 0)
    def _():
        s_in[...] = jnp.zeros_like(s_in)
        tile_in[...] = jnp.full((8, HD), -1.0, F32)

    @pl.when(ctx == last)
    def _():
        g_in[...] = jnp.zeros_like(g_in)

    arrived(0)
    arrived(1)
    local_sums(0)
    for x in range(few_f):
        local_sums(many_f + x)

    pl.semaphore_wait(
        barrier,
        ndp + jnp.where(ctx > 0, 1, 0) + jnp.where(ctx < last, 1, 0),
    )

    @pl.when(ctx < last)
    def _():
        tile_copy().start()

    first_send(0)

    if few_f:
        @pl.when(ctx == 1)
        def _():
            for x in range(few_f):
                early_f(x).start()

    @pl.loop(1, many_f)
    def _(h):
        local_sums(h)
        first_send(h)

    for x in range(few_f):
        first_send(many_f + x)

    arrived(2)
    turn_f = jnp.where(ctx == last, many_f, 0)
    for j in range(blocks):
        scores(lax.rem(turn_f, heads), j)
    gain_copy.wait()
    arrived(3)

    @pl.when(ctx > 0)
    def _():
        tile_copy().wait_recv()

    first = jnp.full((1, HD), seg[0][0], jnp.int32).astype(F32)
    match = flag(tile_in[0:1, :] == first)
    at0 = rows_of(0)
    mprev[at0, :] = (mprev[at0, :].astype(F32) * match).astype(BF16)
    reach = [match * step[0]]
    for j in range(1, blocks):
        reach.append(reach[-1] * step[j])

    if few_f:
        @pl.when(ctx == 2)
        def _():
            for x in range(few_f):
                h = many_f + x
                early_f(x).wait_recv()
                local[h, blocks - 1] = local[h, blocks - 1] + s_early[x] * reach[-1]
                for p in range(PARTS_F):
                    fwd_copy(h, p).start()

    def take_state(h, p):
        at = part(p, PARTS_F)

        @pl.when(ctx > 0)
        def _():
            fwd_copy(h, p).wait_recv()

        @pl.when(jnp.logical_and(inner, h < many_f))
        def _():
            local[h, blocks - 1, at, :] = (
                local[h, blocks - 1, at, :] + s_in[h, at, :] * reach[-1]
            )
            fwd_copy(h, p).start()

        if few_f:
            @pl.when(jnp.logical_and(inner, h >= many_f))
            def _():
                x = h - many_f

                @pl.when(ctx == 1)
                def _():
                    s_early[x, at, :] = s_in[h, at, :] * reach[-1]
                    fwd_copy(h, p, s_early.at[x]).start()

                @pl.when(ctx == 2)
                def _():
                    s_in[h, at, :] = s_in[h, at, :] + s_early[x, at, :]

    def attend(h):
        gain = gain_ref[pl.ds(h, 1), :]
        came = s_in[h]
        for j in range(blocks):
            at = rows_of(j)
            state = came if j == 0 else local[h, j - 1] + came * reach[j - 1]
            state = state.astype(BF16)
            state_bf[h, j] = state
            a = att[h, at, :] + nn(qs[h, at, :] * mprev[at, :], state)
            att[h, at, :] = a
            sq_acc[at, :] += a * a
            in_acc[at, :] += a * (gs[h, at, :].astype(F32) * gain)

    @pl.loop(0, heads - 1)
    def _(i):
        h = lax.rem(i + turn_f, heads)
        after = lax.rem(h + 1, heads)

        def piece(n):
            if n < blocks:
                scores(after, n)
            else:
                attend(h)

        interleave(PARTS_F, functools.partial(take_state, h), piece)

    final = lax.rem(heads - 1 + turn_f, heads)
    for p in range(PARTS_F):
        take_state(final, p)
    attend(final)

    ones = jnp.ones((16, HD), BF16)
    for n, acc in ((0, sq_acc), (1, in_acc)):
        whole = acc[...]
        high = whole.astype(BF16)
        low = (whole - high.astype(F32)).astype(BF16)
        sums_out[n] = (nt(ones, high) + nt(ones, low))[0:8, :]
    swap = pltpu.make_async_remote_copy(
        sums_out, sums_in, xs_sem, xr_sem, device_id={"tensor": 1 - ten}, device_id_type=MESH
    )
    swap.start()
    swap.wait_recv()
    total_sq = sums_out[0] + sums_in[0]
    total_in = sums_out[1] + sums_in[1]
    radius = jnp.sqrt(total_sq / width + 1e-06)
    inv = 1.0 / radius
    level = lax.broadcasted_iota(jnp.int32, (8, toks), 0)
    for acc, row in ((sq_acc, inv), (in_acc, total_in / (width * radius * radius) * inv)):
        high = row.astype(BF16).astype(F32)
        low = row - high
        middle = low.astype(BF16).astype(F32)
        split = jnp.where(level == 0, high, jnp.where(level == 1, middle, low - middle))
        split = jnp.where(level < 3, split, 0.0)
        split = jnp.concatenate([split, jnp.zeros_like(split)], axis=0).astype(BF16)
        acc[...] = tn(split, ones)

    keep = [match * step[0]] + step[1:]
    full = [None] * (blocks + 1)
    full[blocks] = 1.0
    for j in reversed(range(blocks)):
        full[j] = full[j + 1] * keep[j]

    first_rest = min(many_b, 5)

    @pl.loop(0, heads)
    def _(i):
        h = lax.rem(i + jnp.where(ctx == 2, many_b, 0), heads)
        gain = gain_ref[pl.ds(h, 1), :]
        total = jnp.zeros((1, HD), F32)
        adds = []
        for j in range(blocks):
            at = rows_of(j)
            inv = sq_acc[at, :]
            a = att[h, at, :]
            g = gs[h, at, :].astype(F32)
            total = total + jnp.sum(g * (a * inv), axis=0, keepdims=True)
            d = (g * gain * inv - a * in_acc[at, :]).astype(BF16)
            gs[h, at, :] = d
            adds.append(tn(qs[h, at, :] * mprev[at, :], d))
        gg_part[pl.ds(h, 1), :] = total
        run = None
        for j in reversed(range(blocks)):
            run = adds[j] if run is None else adds[j] + run * keep[j]
            grad_local[h, j] = run

        @pl.when(jnp.logical_and(ctx == last, jnp.logical_and(ctx > 0, h < first_rest)))
        def _():
            for p in range(PARTS_B):
                bwd_copy(h, p).start()

        if few_b:
            @pl.when(jnp.logical_and(ctx == 2, h >= many_b))
            def _():
                early_b(h - many_b).start()

        for j in range(blocks):
            at = rows_of(j)
            no_s[h, at, :] = (att[h, at, :] * sq_acc[at, :] * gain).astype(BF16)

    def dp_copy(to, slot):
        return pltpu.make_async_remote_copy(
            gg_part, gg_dp.at[slot], ds_sem, dr_sem.at[slot],
            device_id={"dp": to}, device_id_type=MESH,
        )

    gg_dp[dp] = gg_part[...]

    @pl.loop(1, ndp)
    def _(d):
        dp_copy(lax.rem(dp + d, ndp), dp).start()

    def down_copy():
        return pltpu.make_async_remote_copy(
            gg_down_out, gg_down_in, cs_sem.at[0], cr_sem.at[0], device_id=below, device_id_type=MESH
        )

    def up_copy():
        return pltpu.make_async_remote_copy(
            gg_up_out, gg_up_in, cs_sem.at[1], cr_sem.at[1], device_id=above, device_id_type=MESH
        )

    def take_grad(h, p):
        at = part(p, PARTS_B)

        @pl.when(ctx < last)
        def _():
            bwd_copy(h, p).wait_recv()

        @pl.when(jnp.logical_and(inner, h < many_b))
        def _():
            grad_local[h, 0, at, :] = grad_local[h, 0, at, :] + g_in[h, at, :] * full[0]
            bwd_copy(h, p).start()

        if few_b:
            @pl.when(jnp.logical_and(inner, h >= many_b))
            def _():
                x = h - many_b

                @pl.when(ctx == 2)
                def _():
                    g_early[x, at, :] = g_in[h, at, :] * full[0]
                    bwd_copy(h, p, g_early.at[x]).start()

                @pl.when(ctx == 1)
                def _():
                    g_in[h, at, :] = g_in[h, at, :] + g_early[x, at, :]

    def send_down():
        @pl.when(inner)
        def _():
            down_copy().wait_recv()
            gg_down_out[...] = gg_own[...] + gg_down_in[...]

        @pl.when(jnp.logical_and(ctx > 0, ctx == last))
        def _():
            gg_down_out[...] = gg_own[...]

        @pl.when(ctx > 0)
        def _():
            down_copy().start()

        @pl.when(jnp.logical_and(ctx > 0, ctx == last))
        def _():
            for h in range(first_rest, heads):
                for p in range(PARTS_B):
                    bwd_copy(h, p).start()

    lag = jnp.where(ctx == 0, heads, jnp.clip(2 * (last - ctx) - 1, 0, heads))
    turn_b = jnp.where(ctx == 0, many_b, 0)
    own_at = jnp.where(ctx == last, min(2, heads - 1), min(3, heads - 1))
    down_at = jnp.where(ctx == last, -1, lag + first_rest - 1)
    up_at = jnp.clip(3 * ctx, 3, heads + lag - 1)

    @pl.loop(0, heads + lag)
    def _(i):
        done = lax.rem(jnp.maximum(i - lag, 0) + turn_b, heads)

        if few_b:
            @pl.when(jnp.logical_and(ctx == 1, i == lag))
            def _():
                for x in range(few_b):
                    h = many_b + x
                    early_b(x).wait_recv()
                    grad_local[h, 0] = grad_local[h, 0] + g_early[x] * full[0]
                    for p in range(PARTS_B):
                        bwd_copy(h, p).start()

        @pl.when(i == own_at)
        def _():
            @pl.loop(1, ndp)
            def _(d):
                peer = lax.rem(dp + d, ndp)
                dp_copy(peer, peer).wait_recv()

            own = gg_dp[0]
            for n in range(1, ndp):
                own = own + gg_dp[n]
            gg_own[...] = own

        pl.when(jnp.logical_and(i == own_at, ctx == last))(send_down)

        def take(p):
            @pl.when(i >= lag)
            def _():
                take_grad(done, p)

        def intra(j):
            @pl.when(i < heads)
            def _():
                h = i
                at = rows_of(j)
                d = gs[h, at, :]
                dw = (nt(d, vs[h, at, :]) * visible[j]).astype(BF16)
                gq = nn(dw, ks[h, at, :]) + nt(d * mprev[at, :], state_bf[h, j])
                gq_s[h, at, :] = gq.astype(BF16)
                dw_t = (nt(vs[h, at, :], d) * visible_t[j]).astype(BF16)
                att[h, at, :] = nn(dw_t, qs[h, at, :])
                gv_part[h, at, :] = nn(weights_t[h, j], d)

        def finish():
            h = done
            came = g_in[h]
            for j in range(blocks):
                at = rows_of(j)
                grad = came if j == blocks - 1 else grad_local[h, j + 1] + came * full[j + 1]
                grad = grad.astype(BF16)
                ml = mlast[at, :]
                gk_s[h, at, :] = (att[h, at, :] + nt(vs[h, at, :] * ml, grad)).astype(BF16)
                gv_s[h, at, :] = (gv_part[h, at, :] + nn(ks[h, at, :] * ml, grad)).astype(BF16)

        def piece(n):
            if n < blocks:
                intra(n)
            else:
                pl.when(i == down_at)(send_down)
                pl.when(i >= lag)(finish)

        interleave(PARTS_B, take, piece)

        @pl.when(jnp.logical_and(i == up_at, ctx < last))
        def _():
            @pl.when(ctx > 0)
            def _():
                up_copy().wait_recv()
                gg_up_out[...] = gg_own[...] + gg_up_in[...]

            @pl.when(ctx == 0)
            def _():
                gg_up_out[...] = gg_own[...]

            up_copy().start()

    @pl.when(ctx == 0)
    def _():
        @pl.when(ctx < last)
        def _():
            down_copy().wait_recv()
            gg_ref[...] = gg_own[...] + gg_down_in[...]

        @pl.when(ctx == last)
        def _():
            gg_ref[...] = gg_own[...]

    @pl.when(inner)
    def _():
        gg_ref[...] = gg_up_out[...] + gg_down_in[...]

    @pl.when(jnp.logical_and(ctx > 0, ctx == last))
    def _():
        up_copy().wait_recv()
        gg_ref[...] = gg_up_in[...] + gg_own[...]

    swap.wait_send()
    pltpu.make_async_remote_copy(
        gg_dp.at[pl.ds(0, ndp - 1)], gg_dp.at[pl.ds(0, ndp - 1)], ds_sem, dr_sem.at[0],
        device_id={"dp": dp}, device_id_type=MESH,
    ).wait_send()

    @pl.when(ctx < last)
    def _():
        tile_copy().wait_send()
        up_copy().wait_send()
        pltpu.make_async_remote_copy(
            s_in, s_in, fs_sem, fr_sem.at[0], device_id=above, device_id_type=MESH
        ).wait_send()

    if few_f:
        @pl.when(ctx == 1)
        def _():
            pltpu.make_async_remote_copy(
                s_early, s_early, es_sem.at[0], ef_sem.at[0], device_id=above, device_id_type=MESH
            ).wait_send()

    if few_b:
        @pl.when(ctx == 2)
        def _():
            pltpu.make_async_remote_copy(
                g_early, g_early, es_sem.at[1], eb_sem.at[0], device_id=below, device_id_type=MESH
            ).wait_send()

    @pl.when(ctx > 0)
    def _():
        down_copy().wait_send()
        pltpu.make_async_remote_copy(
            g_in, g_in, bs_sem, br_sem.at[0], device_id=below, device_id_type=MESH
        ).wait_send()


def writer(heads, *refs):
    sems, gain_sem = refs[10:]
    small = pltpu.make_async_copy(refs[4], refs[9], gain_sem)
    small.start()

    def copy(n, h):
        cols = pl.ds(pl.multiple_of(h * HD, HD), HD)
        return pltpu.make_async_copy(refs[n].at[h], refs[5 + n].at[0, :, cols], sems.at[n])

    @pl.loop(0, heads)
    def _(h):
        for n in range(4):
            copy(n, h).start()

    for n in range(4):
        pltpu.make_async_copy(refs[n], refs[n], sems.at[n]).wait()

    small.wait()


def body(nctx, ndp, full_width, queries, keys_in, values, norm_gain, segment_ids, grad_out):
    toks, local_width = queries.shape[1:]
    heads = local_width // HD
    blocks = toks // BLK
    wide = jax.ShapeDtypeStruct(queries.shape, BF16)
    hbm = pl.BlockSpec(memory_space=pl.ANY)
    vmem = pl.BlockSpec(memory_space=pltpu.VMEM)
    per_head = pltpu.VMEM((heads, toks, HD), BF16)
    states = pltpu.VMEM((heads, blocks, HD, HD), F32)
    hops = pltpu.VMEM((heads, HD, HD), F32)
    ids = segment_ids.shape[1]
    short = nctx == 4 and 2 * ids + 2 > nctx * ids // 2
    few_f, few_b = (EARLY_F, EARLY_B) if short else (0, 0)

    def early(few):
        return pltpu.VMEM((max(few, 1), HD, HD), F32)

    rowish = pltpu.VMEM((toks, HD), F32)
    dma = pltpu.SemaphoreType.DMA
    sums = pltpu.VMEM((2, 8, toks), F32)
    tile = pltpu.VMEM((8, HD), F32)
    gains = pltpu.VMEM((heads, HD), F32)
    outs = pl.pallas_call(
        functools.partial(kernel, nctx, ndp, heads, blocks, full_width, few_f, few_b),
        out_shape=[pltpu.VMEM((heads, toks, HD), BF16)] * 4 + [pltpu.VMEM((heads, HD), F32)],
        in_specs=[hbm] * 6,
        out_specs=[vmem] * 5,
        scratch_shapes=[pltpu.SMEM(segment_ids.shape, jnp.int32), gains]
        + [per_head] * 4
        + [
            pltpu.VMEM((heads, toks, HD), F32),
            pltpu.VMEM((heads, toks, HD), F32),
            pltpu.VMEM((heads, blocks, BLK, BLK), BF16),
            pltpu.VMEM((blocks, BLK, BLK), F32),
            pltpu.VMEM((blocks, BLK, BLK), F32),
            pltpu.VMEM((toks, HD), BF16),
            pltpu.VMEM((toks, HD), BF16),
            states,
            pltpu.VMEM((heads, blocks, HD, HD), BF16),
            hops, early(few_f), states, hops, early(few_b),
            rowish, rowish,
            tile, tile, sums, sums,
            gains, pltpu.VMEM((ndp, heads, HD), F32),
            gains, gains, gains, gains, gains, tile,
            dma((6,)),
            dma, dma((heads * PARTS_F,)), dma, dma((heads * PARTS_B,)),
            dma((2,)), dma((max(few_f, 1),)), dma((max(few_b, 1),)),
            dma, dma, dma, dma,
            dma, dma((ndp,)), dma((2,)), dma((2,)),
        ],
        compiler_params=pltpu.CompilerParams(
            collective_id=0, has_side_effects=True, vmem_limit_bytes=55 << 20
        ),
    )(segment_ids, norm_gain.reshape(heads, HD), queries, keys_in, values, grad_out)
    copies = pl.pallas_call(
        functools.partial(writer, heads),
        out_shape=[wide] * 4 + [jax.ShapeDtypeStruct((heads, HD), F32)],
        in_specs=[hbm] * 5,
        out_specs=[hbm] * 5,
        scratch_shapes=[dma((4,)), dma],
        compiler_params=pltpu.CompilerParams(vmem_limit_bytes=1 << 20),
    )(*outs)
    return (*copies[:4], copies[4].reshape(local_width))


def solution(mesh):
    wide = P("dp", "context", "tensor")
    in_specs = (wide, wide, wide, P("tensor"), P("dp", "context"), wide)
    out_specs = (wide, wide, wide, wide, P("tensor"))

    def run(queries, *rest):
        fn = functools.partial(
            body, mesh.shape["context"], mesh.shape["dp"], queries.shape[2]
        )
        return jax.shard_map(
            fn, mesh=mesh, in_specs=in_specs, out_specs=out_specs, check_vma=False
        )(queries, *rest)

    return run
```

```python
import functools

import jax
import jax.numpy as jnp
from jax import lax
from jax.experimental import pallas as pl
from jax.experimental.pallas import tpu as pltpu
from jax.sharding import PartitionSpec as P

HD = 128
BLK = 256
SEGB = 64
PARTS_F = 2
PARTS_B = 1
EARLY_F = 2
EARLY_B = 3
PER = BLK // SEGB
F32 = jnp.float32
BF16 = jnp.bfloat16
MESH = pl.DeviceIdType.MESH


def nn(a, b):
    return lax.dot_general(a, b, (((1,), (0,)), ((), ())), preferred_element_type=F32)


def nt(a, b):
    return lax.dot_general(a, b, (((1,), (1,)), ((), ())), preferred_element_type=F32)


def tn(a, b):
    return lax.dot_general(a, b, (((0,), (0,)), ((), ())), preferred_element_type=F32)


def flag(cond):
    return jnp.where(cond, 1.0, 0.0).astype(F32)


def spread(index, ids):
    out = jnp.full(index.shape, ids[-1], jnp.int32)
    for i in reversed(range(len(ids) - 1)):
        out = jnp.where(index < (i + 1) * SEGB, ids[i], out)
    return out


def kernel(
    nctx, ndp, heads, blocks, width, few_f, few_b,
    seg_hbm, gain_hbm, q_hbm, k_hbm, v_hbm, g_hbm,
    no_s, gq_s, gk_s, gv_s, gg_ref,
    seg_ref, gain_ref, qs, ks, vs, gs,
    att, gv_part, weights_t, visible, visible_t, mprev, mlast,
    local, state_bf, s_in, s_early, grad_local, g_in, g_early,
    sq_acc, in_acc, tile_out, tile_in, sums_out, sums_in,
    gg_part, gg_dp, gg_own, gg_down_out, gg_down_in, gg_up_out, gg_up_in, match_ref,
    in_sem, fs_sem, fr_sem, bs_sem, br_sem, es_sem, ef_sem, eb_sem, ts_sem, tr_sem,
    xs_sem, xr_sem, ds_sem, dr_sem, cs_sem, cr_sem,
):
    ctx = lax.axis_index("context")
    ten = lax.axis_index("tensor")
    dp = lax.axis_index("dp")
    toks = blocks * BLK
    last = nctx - 1
    below = {"context": jnp.maximum(ctx - 1, 0)}
    above = {"context": jnp.minimum(ctx + 1, last)}
    inner = jnp.logical_and(ctx > 0, ctx < last)
    many_f, many_b = heads - few_f, heads - few_b

    barrier = pltpu.get_barrier_semaphore()

    @pl.when(ctx > 0)
    def _():
        pl.semaphore_signal(barrier, inc=1, device_id=below, device_id_type=MESH)

    @pl.when(ctx < last)
    def _():
        pl.semaphore_signal(barrier, inc=1, device_id=above, device_id_type=MESH)

    pl.semaphore_signal(barrier, inc=1, device_id={"tensor": 1 - ten}, device_id_type=MESH)

    @pl.loop(1, ndp)
    def _(d):
        pl.semaphore_signal(
            barrier, inc=1, device_id={"dp": lax.rem(dp + d, ndp)}, device_id_type=MESH
        )

    seg_copy = pltpu.make_async_copy(seg_hbm, seg_ref, in_sem.at[4])
    gain_copy = pltpu.make_async_copy(gain_hbm, gain_ref, in_sem.at[5])
    seg_copy.start()
    gain_copy.start()

    ins = ((k_hbm, ks), (v_hbm, vs), (q_hbm, qs), (g_hbm, gs))

    def load(n, h, sem):
        src, dst = ins[n]
        cols = pl.ds(pl.multiple_of(h * HD, HD), HD)
        pltpu.make_async_copy(src.at[0, :, cols], dst.at[h], in_sem.at[sem]).start()

    for n in range(4):
        @pl.loop(0, heads)
        def _(h):
            load(n, h, n)

    def arrived(n):
        pltpu.make_async_copy(ins[n][1], ins[n][1], in_sem.at[n]).wait()

    seg_copy.wait()
    seg = [[seg_ref[0, j * PER + i] for i in range(PER)] for j in range(blocks)]
    lasts = [seg[j][-1] for j in range(blocks)]
    tile_out[...] = jnp.full((8, HD), lasts[-1], jnp.int32).astype(F32)
    rows_h = lax.broadcasted_iota(jnp.int32, (BLK, HD), 0)
    step = [flag(seg[0][0] == lasts[0])]
    for j in range(1, blocks):
        step.append(flag(lasts[j - 1] == lasts[j]))

    def rows_of(j):
        return pl.ds(j * BLK, BLK)

    for j in range(blocks):
        seg_h = spread(rows_h, seg[j])
        mlast[rows_of(j), :] = flag(seg_h == lasts[j]).astype(BF16)
        before = seg[0][0] if j == 0 else lasts[j - 1]
        mprev[rows_of(j), :] = flag(seg_h == before).astype(BF16)

    def tile_copy():
        return pltpu.make_async_remote_copy(
            tile_out, tile_in, ts_sem, tr_sem, device_id=above, device_id_type=MESH
        )

    def part(p, parts):
        return pl.ds(p * (HD // parts), HD // parts)

    def fwd_copy(h, p, src=None):
        src = local.at[h, blocks - 1] if src is None else src
        return pltpu.make_async_remote_copy(
            src.at[part(p, PARTS_F)], s_in.at[h, part(p, PARTS_F)], fs_sem,
            fr_sem.at[h * PARTS_F + p], device_id=above, device_id_type=MESH,
        )

    def bwd_copy(h, p, src=None):
        src = grad_local.at[h, 0] if src is None else src
        return pltpu.make_async_remote_copy(
            src.at[part(p, PARTS_B)], g_in.at[h, part(p, PARTS_B)], bs_sem,
            br_sem.at[h * PARTS_B + p], device_id=below, device_id_type=MESH,
        )

    def early_f(x):
        return pltpu.make_async_remote_copy(
            local.at[many_f + x, blocks - 1], s_early.at[x], es_sem.at[0],
            ef_sem.at[x], device_id=above, device_id_type=MESH,
        )

    def early_b(x):
        return pltpu.make_async_remote_copy(
            grad_local.at[many_b + x, 0], g_early.at[x], es_sem.at[1],
            eb_sem.at[x], device_id=below, device_id_type=MESH,
        )

    def local_sums(h):
        run = None
        for j in range(blocks):
            km = ks[h, rows_of(j), :] * mlast[rows_of(j), :]
            add = tn(km, vs[h, rows_of(j), :])
            run = add if run is None else run * step[j] + add
            local[h, j] = run

    def scores(h, j):
        at = rows_of(j)
        w = (nt(qs[h, at, :], ks[h, at, :]) * visible[j]).astype(BF16)
        w_t = nt(ks[h, at, :], qs[h, at, :]) * visible_t[j]
        weights_t[h, j] = w_t.astype(BF16)
        att[h, at, :] = nn(w, vs[h, at, :])

    def interleave(parts, take, piece):
        for n in range(blocks + 1):
            for p in range(parts):
                if p * (blocks + 1) // parts == n:
                    take(p)
            piece(n)

    def first_send(h):
        @pl.when(jnp.logical_and(ctx == 0, ctx < last))
        def _():
            for p in range(PARTS_F):
                fwd_copy(h, p).start()

    rows = lax.broadcasted_iota(jnp.int32, (BLK, BLK), 0)
    cols = lax.broadcasted_iota(jnp.int32, (BLK, BLK), 1)
    for j in range(blocks):
        same = spread(rows, seg[j]) == spread(cols, seg[j])
        visible[j] = flag(jnp.logical_and(rows >= cols, same))
        visible_t[j] = flag(jnp.logical_and(cols >= rows, same))
    sq_acc[...] = jnp.zeros_like(sq_acc)
    in_acc[...] = jnp.zeros_like(in_acc)

    @pl.when(ctx == 0)
    def _():
        s_in[...] = jnp.zeros_like(s_in)
        tile_in[...] = jnp.full((8, HD), -1.0, F32)

    @pl.when(ctx == last)
    def _():
        g_in[...] = jnp.zeros_like(g_in)

    arrived(0)
    arrived(1)
    local_sums(0)
    for x in range(few_f):
        local_sums(many_f + x)

    pl.semaphore_wait(
        barrier,
        ndp + jnp.where(ctx > 0, 1, 0) + jnp.where(ctx < last, 1, 0),
    )

    @pl.when(ctx < last)
    def _():
        tile_copy().start()

    first_send(0)

    if few_f:
        @pl.when(ctx == 1)
        def _():
            for x in range(few_f):
                early_f(x).start()

    @pl.loop(1, many_f)
    def _(h):
        local_sums(h)
        first_send(h)

    for x in range(few_f):
        first_send(many_f + x)

    arrived(2)
    turn_f = jnp.where(ctx == last, many_f, 0)
    for j in range(blocks):
        scores(lax.rem(turn_f, heads), j)
    gain_copy.wait()
    arrived(3)

    @pl.when(ctx > 0)
    def _():
        tile_copy().wait_recv()

    first = jnp.full((1, HD), seg[0][0], jnp.int32).astype(F32)
    match = flag(tile_in[0:1, :] == first)
    at0 = rows_of(0)
    mprev[at0, :] = (mprev[at0, :].astype(F32) * match).astype(BF16)
    reach = [match * step[0]]
    for j in range(1, blocks):
        reach.append(reach[-1] * step[j])

    if few_f:
        @pl.when(ctx == 2)
        def _():
            for x in range(few_f):
                h = many_f + x
                early_f(x).wait_recv()
                local[h, blocks - 1] = local[h, blocks - 1] + s_early[x] * reach[-1]
                for p in range(PARTS_F):
                    fwd_copy(h, p).start()

    def take_state(h, p):
        at = part(p, PARTS_F)

        @pl.when(ctx > 0)
        def _():
            fwd_copy(h, p).wait_recv()

        @pl.when(jnp.logical_and(inner, h < many_f))
        def _():
            local[h, blocks - 1, at, :] = (
                local[h, blocks - 1, at, :] + s_in[h, at, :] * reach[-1]
            )
            fwd_copy(h, p).start()

        if few_f:
            @pl.when(jnp.logical_and(inner, h >= many_f))
            def _():
                x = h - many_f

                @pl.when(ctx == 1)
                def _():
                    s_early[x, at, :] = s_in[h, at, :] * reach[-1]
                    fwd_copy(h, p, s_early.at[x]).start()

                @pl.when(ctx == 2)
                def _():
                    s_in[h, at, :] = s_in[h, at, :] + s_early[x, at, :]

    def attend(h):
        gain = gain_ref[pl.ds(h, 1), :]
        came = s_in[h]
        for j in range(blocks):
            at = rows_of(j)
            state = came if j == 0 else local[h, j - 1] + came * reach[j - 1]
            state = state.astype(BF16)
            state_bf[h, j] = state
            a = att[h, at, :] + nn(qs[h, at, :] * mprev[at, :], state)
            att[h, at, :] = a
            sq_acc[at, :] += a * a
            in_acc[at, :] += a * (gs[h, at, :].astype(F32) * gain)

    @pl.loop(0, heads - 1)
    def _(i):
        h = lax.rem(i + turn_f, heads)
        after = lax.rem(h + 1, heads)

        def piece(n):
            if n < blocks:
                scores(after, n)
            else:
                attend(h)

        interleave(PARTS_F, functools.partial(take_state, h), piece)

    final = lax.rem(heads - 1 + turn_f, heads)
    for p in range(PARTS_F):
        take_state(final, p)
    attend(final)

    ones = jnp.ones((16, HD), BF16)
    for n, acc in ((0, sq_acc), (1, in_acc)):
        whole = acc[...]
        high = whole.astype(BF16)
        low = (whole - high.astype(F32)).astype(BF16)
        both = jnp.concatenate([high, low], axis=1)
        sums_out[n] = nt(jnp.ones((16, 2 * HD), BF16), both)[0:8, :]
    swap = pltpu.make_async_remote_copy(
        sums_out, sums_in, xs_sem, xr_sem, device_id={"tensor": 1 - ten}, device_id_type=MESH
    )
    swap.start()
    swap.wait_recv()
    total_sq = sums_out[0] + sums_in[0]
    total_in = sums_out[1] + sums_in[1]
    radius = jnp.sqrt(total_sq / width + 1e-06)
    inv = 1.0 / radius
    level = lax.broadcasted_iota(jnp.int32, (8, toks), 0)
    for acc, row in ((sq_acc, inv), (in_acc, total_in / (width * radius * radius) * inv)):
        high = row.astype(BF16).astype(F32)
        low = row - high
        middle = low.astype(BF16).astype(F32)
        split = jnp.where(level == 0, high, jnp.where(level == 1, middle, low - middle))
        split = jnp.where(level < 3, split, 0.0)
        split = jnp.concatenate([split, jnp.zeros_like(split)], axis=0).astype(BF16)
        acc[...] = tn(split, ones)

    keep = [match * step[0]] + step[1:]
    full = [None] * (blocks + 1)
    full[blocks] = 1.0
    for j in reversed(range(blocks)):
        full[j] = full[j + 1] * keep[j]

    first_rest = min(many_b, 5)

    @pl.loop(0, heads)
    def _(i):
        h = lax.rem(i + jnp.where(ctx == 2, many_b, 0), heads)
        gain = gain_ref[pl.ds(h, 1), :]
        total = jnp.zeros((1, HD), F32)
        adds = []
        for j in range(blocks):
            at = rows_of(j)
            inv = sq_acc[at, :]
            a = att[h, at, :]
            g = gs[h, at, :].astype(F32)
            total = total + jnp.sum(g * (a * inv), axis=0, keepdims=True)
            d = (g * gain * inv - a * in_acc[at, :]).astype(BF16)
            gs[h, at, :] = d
            adds.append(tn(qs[h, at, :] * mprev[at, :], d))
        gg_part[pl.ds(h, 1), :] = total
        run = None
        for j in reversed(range(blocks)):
            run = adds[j] if run is None else adds[j] + run * keep[j]
            grad_local[h, j] = run

        @pl.when(jnp.logical_and(ctx == last, jnp.logical_and(ctx > 0, h < first_rest)))
        def _():
            for p in range(PARTS_B):
                bwd_copy(h, p).start()

        if few_b:
            @pl.when(jnp.logical_and(ctx == 2, h >= many_b))
            def _():
                early_b(h - many_b).start()

        for j in range(blocks):
            at = rows_of(j)
            no_s[h, at, :] = (att[h, at, :] * sq_acc[at, :] * gain).astype(BF16)

    def dp_copy(to, slot):
        return pltpu.make_async_remote_copy(
            gg_part, gg_dp.at[slot], ds_sem, dr_sem.at[slot],
            device_id={"dp": to}, device_id_type=MESH,
        )

    gg_dp[dp] = gg_part[...]

    @pl.loop(1, ndp)
    def _(d):
        dp_copy(lax.rem(dp + d, ndp), dp).start()

    def down_copy():
        return pltpu.make_async_remote_copy(
            gg_down_out, gg_down_in, cs_sem.at[0], cr_sem.at[0], device_id=below, device_id_type=MESH
        )

    def up_copy():
        return pltpu.make_async_remote_copy(
            gg_up_out, gg_up_in, cs_sem.at[1], cr_sem.at[1], device_id=above, device_id_type=MESH
        )

    def take_grad(h, p):
        at = part(p, PARTS_B)

        @pl.when(ctx < last)
        def _():
            bwd_copy(h, p).wait_recv()

        @pl.when(jnp.logical_and(inner, h < many_b))
        def _():
            grad_local[h, 0, at, :] = grad_local[h, 0, at, :] + g_in[h, at, :] * full[0]
            bwd_copy(h, p).start()

        if few_b:
            @pl.when(jnp.logical_and(inner, h >= many_b))
            def _():
                x = h - many_b

                @pl.when(ctx == 2)
                def _():
                    g_early[x, at, :] = g_in[h, at, :] * full[0]
                    bwd_copy(h, p, g_early.at[x]).start()

                @pl.when(ctx == 1)
                def _():
                    g_in[h, at, :] = g_in[h, at, :] + g_early[x, at, :]

    def send_down():
        @pl.when(inner)
        def _():
            down_copy().wait_recv()
            gg_down_out[...] = gg_own[...] + gg_down_in[...]

        @pl.when(jnp.logical_and(ctx > 0, ctx == last))
        def _():
            gg_down_out[...] = gg_own[...]

        @pl.when(ctx > 0)
        def _():
            down_copy().start()

        @pl.when(jnp.logical_and(ctx > 0, ctx == last))
        def _():
            for h in range(first_rest, heads):
                for p in range(PARTS_B):
                    bwd_copy(h, p).start()

    lag = jnp.where(ctx == 0, heads, jnp.clip(2 * (last - ctx) - 1, 0, heads))
    turn_b = jnp.where(ctx == 0, many_b, 0)
    own_at = jnp.where(ctx == last, min(2, heads - 1), min(3, heads - 1))
    down_at = jnp.where(ctx == last, -1, lag + first_rest - 1)
    up_at = jnp.clip(3 * ctx, 3, heads + lag - 1)

    @pl.loop(0, heads + lag)
    def _(i):
        done = lax.rem(jnp.maximum(i - lag, 0) + turn_b, heads)

        if few_b:
            @pl.when(jnp.logical_and(ctx == 1, i == lag))
            def _():
                for x in range(few_b):
                    h = many_b + x
                    early_b(x).wait_recv()
                    grad_local[h, 0] = grad_local[h, 0] + g_early[x] * full[0]
                    for p in range(PARTS_B):
                        bwd_copy(h, p).start()

        @pl.when(i == own_at)
        def _():
            @pl.loop(1, ndp)
            def _(d):
                peer = lax.rem(dp + d, ndp)
                dp_copy(peer, peer).wait_recv()

            own = gg_dp[0]
            for n in range(1, ndp):
                own = own + gg_dp[n]
            gg_own[...] = own

        pl.when(jnp.logical_and(i == own_at, ctx == last))(send_down)

        def take(p):
            @pl.when(i >= lag)
            def _():
                take_grad(done, p)

        def intra(j):
            @pl.when(i < heads)
            def _():
                h = i
                at = rows_of(j)
                d = gs[h, at, :]
                dw = (nt(d, vs[h, at, :]) * visible[j]).astype(BF16)
                gq = nn(dw, ks[h, at, :]) + nt(d * mprev[at, :], state_bf[h, j])
                gq_s[h, at, :] = gq.astype(BF16)
                dw_t = (nt(vs[h, at, :], d) * visible_t[j]).astype(BF16)
                att[h, at, :] = nn(dw_t, qs[h, at, :])
                gv_part[h, at, :] = nn(weights_t[h, j], d)

        def finish():
            h = done
            came = g_in[h]
            for j in range(blocks):
                at = rows_of(j)
                grad = came if j == blocks - 1 else grad_local[h, j + 1] + came * full[j + 1]
                grad = grad.astype(BF16)
                ml = mlast[at, :]
                gk_s[h, at, :] = (att[h, at, :] + nt(vs[h, at, :] * ml, grad)).astype(BF16)
                gv_s[h, at, :] = (gv_part[h, at, :] + nn(ks[h, at, :] * ml, grad)).astype(BF16)

        def piece(n):
            if n < blocks:
                intra(n)
            else:
                pl.when(i == down_at)(send_down)
                pl.when(i >= lag)(finish)

        interleave(PARTS_B, take, piece)

        @pl.when(jnp.logical_and(i == up_at, ctx < last))
        def _():
            @pl.when(ctx > 0)
            def _():
                up_copy().wait_recv()
                gg_up_out[...] = gg_own[...] + gg_up_in[...]

            @pl.when(ctx == 0)
            def _():
                gg_up_out[...] = gg_own[...]

            up_copy().start()

    @pl.when(ctx == 0)
    def _():
        @pl.when(ctx < last)
        def _():
            down_copy().wait_recv()
            gg_ref[...] = gg_own[...] + gg_down_in[...]

        @pl.when(ctx == last)
        def _():
            gg_ref[...] = gg_own[...]

    @pl.when(inner)
    def _():
        gg_ref[...] = gg_up_out[...] + gg_down_in[...]

    @pl.when(jnp.logical_and(ctx > 0, ctx == last))
    def _():
        up_copy().wait_recv()
        gg_ref[...] = gg_up_in[...] + gg_own[...]

    swap.wait_send()
    pltpu.make_async_remote_copy(
        gg_dp.at[pl.ds(0, ndp - 1)], gg_dp.at[pl.ds(0, ndp - 1)], ds_sem, dr_sem.at[0],
        device_id={"dp": dp}, device_id_type=MESH,
    ).wait_send()

    @pl.when(ctx < last)
    def _():
        tile_copy().wait_send()
        up_copy().wait_send()
        pltpu.make_async_remote_copy(
            s_in, s_in, fs_sem, fr_sem.at[0], device_id=above, device_id_type=MESH
        ).wait_send()

    if few_f:
        @pl.when(ctx == 1)
        def _():
            pltpu.make_async_remote_copy(
                s_early, s_early, es_sem.at[0], ef_sem.at[0], device_id=above, device_id_type=MESH
            ).wait_send()

    if few_b:
        @pl.when(ctx == 2)
        def _():
            pltpu.make_async_remote_copy(
                g_early, g_early, es_sem.at[1], eb_sem.at[0], device_id=below, device_id_type=MESH
            ).wait_send()

    @pl.when(ctx > 0)
    def _():
        down_copy().wait_send()
        pltpu.make_async_remote_copy(
            g_in, g_in, bs_sem, br_sem.at[0], device_id=below, device_id_type=MESH
        ).wait_send()


def writer(heads, *refs):
    sems, gain_sem = refs[10:]
    small = pltpu.make_async_copy(refs[4], refs[9], gain_sem)
    small.start()

    def copy(n, h):
        cols = pl.ds(pl.multiple_of(h * HD, HD), HD)
        return pltpu.make_async_copy(refs[n].at[h], refs[5 + n].at[0, :, cols], sems.at[n])

    @pl.loop(0, heads)
    def _(h):
        for n in range(4):
            copy(n, h).start()

    for n in range(4):
        pltpu.make_async_copy(refs[n], refs[n], sems.at[n]).wait()

    small.wait()


def body(nctx, ndp, full_width, queries, keys_in, values, norm_gain, segment_ids, grad_out):
    toks, local_width = queries.shape[1:]
    heads = local_width // HD
    blocks = toks // BLK
    wide = jax.ShapeDtypeStruct(queries.shape, BF16)
    hbm = pl.BlockSpec(memory_space=pl.ANY)
    vmem = pl.BlockSpec(memory_space=pltpu.VMEM)
    per_head = pltpu.VMEM((heads, toks, HD), BF16)
    states = pltpu.VMEM((heads, blocks, HD, HD), F32)
    hops = pltpu.VMEM((heads, HD, HD), F32)
    ids = segment_ids.shape[1]
    short = nctx == 4 and 2 * ids + 2 > nctx * ids // 2
    few_f, few_b = (EARLY_F, EARLY_B) if short else (0, 0)

    def early(few):
        return pltpu.VMEM((max(few, 1), HD, HD), F32)

    rowish = pltpu.VMEM((toks, HD), F32)
    dma = pltpu.SemaphoreType.DMA
    sums = pltpu.VMEM((2, 8, toks), F32)
    tile = pltpu.VMEM((8, HD), F32)
    gains = pltpu.VMEM((heads, HD), F32)
    outs = pl.pallas_call(
        functools.partial(kernel, nctx, ndp, heads, blocks, full_width, few_f, few_b),
        out_shape=[pltpu.VMEM((heads, toks, HD), BF16)] * 4 + [pltpu.VMEM((heads, HD), F32)],
        in_specs=[hbm] * 6,
        out_specs=[vmem] * 5,
        scratch_shapes=[pltpu.SMEM(segment_ids.shape, jnp.int32), gains]
        + [per_head] * 4
        + [
            pltpu.VMEM((heads, toks, HD), F32),
            pltpu.VMEM((heads, toks, HD), F32),
            pltpu.VMEM((heads, blocks, BLK, BLK), BF16),
            pltpu.VMEM((blocks, BLK, BLK), F32),
            pltpu.VMEM((blocks, BLK, BLK), F32),
            pltpu.VMEM((toks, HD), BF16),
            pltpu.VMEM((toks, HD), BF16),
            states,
            pltpu.VMEM((heads, blocks, HD, HD), BF16),
            hops, early(few_f), states, hops, early(few_b),
            rowish, rowish,
            tile, tile, sums, sums,
            gains, pltpu.VMEM((ndp, heads, HD), F32),
            gains, gains, gains, gains, gains, tile,
            dma((6,)),
            dma, dma((heads * PARTS_F,)), dma, dma((heads * PARTS_B,)),
            dma((2,)), dma((max(few_f, 1),)), dma((max(few_b, 1),)),
            dma, dma, dma, dma,
            dma, dma((ndp,)), dma((2,)), dma((2,)),
        ],
        compiler_params=pltpu.CompilerParams(
            collective_id=0, has_side_effects=True, vmem_limit_bytes=55 << 20
        ),
    )(segment_ids, norm_gain.reshape(heads, HD), queries, keys_in, values, grad_out)
    copies = pl.pallas_call(
        functools.partial(writer, heads),
        out_shape=[wide] * 4 + [jax.ShapeDtypeStruct((heads, HD), F32)],
        in_specs=[hbm] * 5,
        out_specs=[hbm] * 5,
        scratch_shapes=[dma((4,)), dma],
        compiler_params=pltpu.CompilerParams(vmem_limit_bytes=1 << 20),
    )(*outs)
    return (*copies[:4], copies[4].reshape(local_width))


def solution(mesh):
    wide = P("dp", "context", "tensor")
    in_specs = (wide, wide, wide, P("tensor"), P("dp", "context"), wide)
    out_specs = (wide, wide, wide, wide, P("tensor"))

    def run(queries, *rest):
        fn = functools.partial(
            body, mesh.shape["context"], mesh.shape["dp"], queries.shape[2]
        )
        return jax.shard_map(
            fn, mesh=mesh, in_specs=in_specs, out_specs=out_specs, check_vma=False
        )(queries, *rest)

    return run
```
